32 devices in a mesh: toa: 16 (over z, y, x), rep: 2 (over core).
Axes of the slice: x: 2, y: 2, z: 4, core: 2. Of those that a mesh axis runs over, the one named last changes fastest.
Arguments:
- residual: float32 [2048, 256], P('toa'), may hold values from -6 to 6
- toa_error: float32 [2048, 256], P('toa'), may hold values from 0.3 to 3
- basis_rows: bfloat16 [2048, 100, 256], P('toa', 'rep'), may hold values from -0.041432038 to 0.041432038
- efac_table: float32 [16, 64], replicated, may hold values from 0.5 to 2
- equad_table: float32 [16, 64], replicated, may hold values from 0.1 to 1
- pulsar: int32 [2048], P('toa'), may hold values from 0 to 15
- backend: int32 [2048], P('toa'), may hold values from 0 to 63
- counts: int32 [2048], P('toa'), may hold values from 64 to 256
- owner_slot: int32 [2048], P('toa'), may hold values from 0 to 2047, as said below
Outputs:
- gram_matrix: float32 [16, 100, 100], P('toa', None, 'rep')
- projection: float32 [16, 100], P('toa', 'rep')
- whitened: float32 [2048, 256], P('toa')
The draws below stay inside these ranges and needn't reach their ends.
Inputs may be any that keep to these rules, and one draw needn't show every extreme that they name: A permutation of the 2048 slots, independent of pulsar and backend; owner_slot // 128 is the device index along toa that holds the tile's output row and owner_slot % 128 its place there; each device's tiles go exactly 8 to each device.
All inputs are finite; a program needn't handle non-finite values.
Results may differ from the reference program's by a relative error of at most 0.0032.
Values may be sent and summed in bfloat16 or wider, within the bound.
A program may use at most 64 MiB of HBM per device.

```python
import math
import jax
import jax.numpy as jnp
import numpy as np
from jax import lax

K = 100
B = 64
ROWS = 256
TILES_DEV = 128
PSR_DEV = 1
P_SIZE = 16
TILES = 2048


def draw_basis_rows(key, part):
    noise_key, column_key = jax.random.split(jax.random.fold_in(key, 11))
    spread = 1.0 / math.sqrt(TILES_DEV * ROWS // PSR_DEV)
    noise = jnp.clip(jax.random.normal(noise_key, (TILES, K, ROWS), jnp.float32), -6.0, 6.0)
    column_mean = jax.random.uniform(column_key, (K,), jnp.float32, -1.0, 1.0)
    values = (noise + column_mean[None, :, None]) * spread
    return values.astype(jnp.bfloat16)


def draw_owner_slot(key, part):
    source_key, dest_key = jax.random.split(jax.random.fold_in(key, 23))
    peer_count = TILES // TILES_DEV
    per_peer = TILES_DEV // peer_count
    source_order = jax.vmap(lambda small_key: jax.random.permutation(small_key, TILES_DEV))(jax.random.split(source_key, peer_count))
    dest_order = jax.vmap(lambda small_key: jax.random.permutation(small_key, TILES_DEV))(jax.random.split(dest_key, peer_count))
    source_ids = jnp.arange(peer_count, dtype=jnp.int32)[:, None, None]
    dest_ids = jnp.arange(peer_count, dtype=jnp.int32)[None, :, None]
    copy_ids = jnp.arange(per_peer, dtype=jnp.int32)[None, None, :]
    tile_index = source_ids * TILES_DEV + source_order[source_ids, dest_ids * per_peer + copy_ids]
    slot_value = dest_ids * TILES_DEV + dest_order[dest_ids, source_ids * per_peer + copy_ids]
    tile_index = jnp.broadcast_to(tile_index, (peer_count, peer_count, per_peer)).reshape(-1)
    slot_value = jnp.broadcast_to(slot_value, (peer_count, peer_count, per_peer)).reshape(-1)
    return jnp.zeros((TILES,), jnp.int32).at[tile_index].set(slot_value.astype(jnp.int32))


def touch_ends(array, stream_key, low, top_value):
    spot = [jax.random.randint(jax.random.fold_in(stream_key, axis), (), 0, length) for axis, length in enumerate(array.shape)]
    longest = array.shape.index(max(array.shape))
    next_to = spot[:longest] + [(spot[longest] + 1) % array.shape[longest]] + spot[longest + 1:]
    return array.at[tuple(spot)].set(low).at[tuple(next_to)].set(top_value)


def level_of(key, shape, cuts, smallest, top_value):
    factor_of = 1.0
    for position, blocks in cuts:
        heights = jax.random.uniform(jax.random.fold_in(jax.random.fold_in(key, 6), position), (blocks,), jnp.float32, smallest / len(cuts), top_value / len(cuts))
        factor_of = factor_of * jnp.repeat(jnp.exp(heights), shape[position] // blocks).reshape((-1,) + (1,) * (len(shape) - 1 - position))
    return factor_of


def cumulative_ranks(amount, slope):
    portions = [(1 << 20) // math.isqrt(standing ** slope) + 1 for standing in range(1, amount + 1)]
    width = 1 + sum(portions) // (1 << 30)
    return np.cumsum(np.array([max(1, weight // width) for weight in portions]))


def ranked(stream_key, extent, amount, skew):
    grid = cumulative_ranks(amount, skew)
    pick = jax.random.randint(jax.random.fold_in(stream_key, 1), extent, 0, int(grid[amount - 1]))
    grade = jnp.searchsorted(jnp.asarray(grid, jnp.int32), pick, side="right")
    return jax.random.permutation(jax.random.fold_in(stream_key, 2), amount)[grade].astype(jnp.int32)


def scatter_about(own_key, shape, width, most, cuts=(), kind=jnp.bfloat16):
    loudness = level_of(own_key, shape, cuts, -0.22, 0.18) if cuts else 1.0
    result = jax.random.normal(own_key, shape, jnp.float32) * width * loudness
    return jnp.minimum(jnp.maximum(result, -most), most).astype(kind)


def setup_inputs(seed: int = 0) -> dict:
    splits = jax.random.split(jax.random.key(seed), 10)
    residual = scatter_about(splits[0], (TILES, ROWS), 1.0, 6.0, ((0, 16),), jnp.float32)
    toa_error = jnp.clip(jnp.exp(math.log(3.0) - 2.3025851 * jax.random.uniform(splits[1], (TILES, ROWS), jnp.float32) ** level_of(splits[1], (TILES, ROWS), ((0, 16),), -0.2, 0.2)), 0.3, 3.0)
    basis_rows = draw_basis_rows(jax.random.fold_in(splits[9], 71), 0)
    efac_table = jnp.clip(jnp.exp(jax.random.uniform(splits[3], (P_SIZE, B), jnp.float32, math.log(0.5), math.log(2.0))), 0.5, 2.0)
    equad_table = jnp.clip(jnp.exp(jax.random.uniform(splits[4], (P_SIZE, B), jnp.float32, math.log(0.1), math.log(1.0))), 0.1, 1.0)
    pulsar = touch_ends(ranked(splits[5], (TILES,), P_SIZE, 1), jax.random.fold_in(splits[5], 3), 0, P_SIZE - 1).astype(jnp.int32)
    backend = touch_ends(jax.random.randint(splits[6], (TILES,), 0, B), jax.random.fold_in(splits[6], 1), 0, B - 1).astype(jnp.int32)
    counts = touch_ends(jax.random.randint(splits[7], (TILES,), ROWS // 4, ROWS + 1), jax.random.fold_in(splits[7], 1), ROWS // 4, ROWS).astype(jnp.int32)
    owner_slot = draw_owner_slot(jax.random.fold_in(splits[9], 71), 0)
    return {"residual": residual, "toa_error": toa_error, "basis_rows": basis_rows, "efac_table": efac_table, "equad_table": equad_table, "pulsar": pulsar, "backend": backend, "counts": counts, "owner_slot": owner_slot}


def reference(residual, toa_error, basis_rows, efac_table, equad_table, pulsar, backend, counts, owner_slot):
    factor = efac_table[pulsar, backend]
    floor_term = equad_table[pulsar, backend]
    valid_rows = jnp.arange(ROWS, dtype=jnp.int32)[None, :] < counts[:, None]
    weight = jnp.where(valid_rows, 1.0 / (factor[:, None] ** 2 * toa_error ** 2 + floor_term[:, None] ** 2), 0.0).astype(jnp.float32)
    whitened_local = jnp.sqrt(weight) * residual
    whitened = jnp.zeros_like(whitened_local).at[owner_slot.astype(jnp.int32)].set(whitened_local)
    block_count = TILES // TILES_DEV
    basis_blocks = basis_rows.reshape(block_count, TILES_DEV, K, ROWS)
    weight_blocks = weight.reshape(block_count, TILES_DEV, ROWS)
    residual_blocks = residual.reshape(block_count, TILES_DEV, ROWS)
    pulsar_blocks = pulsar.reshape(block_count, TILES_DEV)
    high = lax.Precision.HIGHEST

    def step_fn(carry, inputs):
        gram_sum, proj_sum = carry
        basis_block, weight_block, residual_block, pulsar_block = inputs
        basis_float = basis_block.astype(jnp.float32)
        scaled = lax.optimization_barrier((weight_block[:, None, :] * basis_float).astype(jnp.bfloat16)).astype(jnp.float32)
        weighted_res = lax.optimization_barrier((weight_block * residual_block).astype(jnp.bfloat16)).astype(jnp.float32)
        tile_gram = jnp.einsum('tkr,tjr->tkj', basis_float, scaled, precision=high)
        tile_proj = jnp.einsum('tkr,tr->tk', basis_float, weighted_res, precision=high)
        onehot = (pulsar_block[:, None] == jnp.arange(P_SIZE, dtype=jnp.int32)[None, :]).astype(jnp.float32)
        gram_sum = gram_sum + jnp.einsum('tp,tkj->pkj', onehot, tile_gram, precision=high)
        proj_sum = proj_sum + jnp.einsum('tp,tk->pk', onehot, tile_proj, precision=high)
        return ((gram_sum, proj_sum), None)
    initial = (jnp.zeros((P_SIZE, K, K), jnp.float32), jnp.zeros((P_SIZE, K), jnp.float32))
    (gram_matrix, projection), unused = lax.scan(step_fn, initial, (basis_blocks, weight_blocks, residual_blocks, pulsar_blocks))
    return (gram_matrix, projection, whitened)
```

```python
import functools

import jax
import jax.numpy as jnp
from jax import lax
from jax.experimental import pallas as pl
from jax.experimental.pallas import tpu as pltpu
from jax.sharding import PartitionSpec as P

MESH = pl.DeviceIdType.MESH
GROUP = 16
LANES = 128
SPAN = LANES // 2
PITCH = GROUP + 1
FOLD = SPAN // 2
PART = FOLD + 1
VMEM_KERNEL = 48 * 1024 * 1024
HIGH = lax.Precision.HIGHEST
SWAP, ROWS, PLACES, OWN, CROSS = range(5)


def round_up(value, step):
    return (value + step - 1) // step * step


def contract(left, right, dims, precision=None):
    return lax.dot_general(
        left, right, (dims, ((), ())), precision=precision, preferred_element_type=jnp.float32
    )


def whole_kernel(
    peers,
    pulsar_hbm,
    backend_hbm,
    counts_hbm,
    slot_hbm,
    efac_hbm,
    equad_hbm,
    residual_hbm,
    error_hbm,
    basis_ref,
    gram_ref,
    projection_ref,
    white_ref,
    pulsar_ref,
    backend_ref,
    counts_ref,
    slot_ref,
    efac_ref,
    equad_ref,
    residual_ref,
    error_ref,
    sorted_rows,
    got_rows,
    sorted_places,
    got_places,
    own_store,
    other_store,
    weights,
    wide_even,
    wide_odd,
    lefts,
    own_grams,
    cross_grams,
    part_wide,
    own_part,
    cross_part,
    got_own,
    got_cross,
    cross_sum,
    partner_sum,
    small_sems,
    load_sems,
    swap_arrivals,
    sends,
    arrivals,
    last_sems,
):
    me = lax.axis_index("toa")
    core = lax.axis_index("rep")
    partner = 1 - core
    half, tile_total, row_total = basis_ref.shape
    pulsar_total = efac_hbm.shape[0]
    owned = pulsar_total // peers
    per_peer = tile_total // peers
    group = min(GROUP, tile_total)
    steps = tile_total // group
    swaps = steps // 2
    cuts = row_total // LANES
    stored = round_up(half + 1, 8)
    apart = stored + 1
    f32 = jnp.float32
    bf16 = jnp.bfloat16

    barrier = pltpu.get_barrier_semaphore()
    pl.semaphore_signal(barrier, inc=1, device_id={"rep": partner}, device_id_type=MESH)

    def each(first, last, action):
        def body(i, carry):
            action(i)
            return carry

        lax.fori_loop(first, last, body, 0)

    def greet(d):
        pl.semaphore_signal(
            barrier, inc=1, device_id={"toa": lax.rem(me + d, peers)}, device_id_type=MESH
        )


    small = [
        pltpu.make_async_copy(source, target, small_sems.at[n])
        for n, (source, target) in enumerate(
            [
                (pulsar_hbm, pulsar_ref),
                (backend_hbm, backend_ref),
                (efac_hbm, efac_ref),
                (equad_hbm, equad_ref),
                (counts_hbm, counts_ref),
                (slot_hbm, slot_ref),
                (error_hbm, error_ref),
                (residual_hbm, residual_ref),
            ]
        )
    ]
    for copy in small:
        copy.start()

    def chunk(ref, g):
        return ref.at[:, pl.ds(pl.multiple_of(g * group, group), group), :]

    def load(g):
        return pltpu.make_async_copy(chunk(basis_ref, g), chunk(own_store, g), load_sems.at[g])

    each(0, steps, lambda g: load(g).start())
    each(1, peers, greet)

    def swap(g):
        return pltpu.make_async_remote_copy(
            src_ref=chunk(basis_ref, partner * swaps + g),
            dst_ref=chunk(other_store, g),
            send_sem=sends.at[SWAP],
            recv_sem=swap_arrivals.at[g],
            device_id={"rep": partner},
            device_id_type=MESH,
        )

    pl.semaphore_wait(barrier, peers)
    each(0, swaps, lambda g: swap(g).start())

    for wide in (wide_even, wide_odd):
        spare = (wide.shape[1] - half * PITCH, LANES)
        for c in range(cuts):
            wide[c, half * PITCH :, :] = jnp.zeros(spare, f32)
    for copy in small:
        copy.wait()

    def onehot(row, amount):
        index = lax.broadcasted_iota(jnp.int32, (amount, row.shape[1]), 0)
        return (index == row).astype(f32)

    def exact(hot, values):
        high = values.astype(bf16)
        rest = values - high.astype(f32)
        middle = rest.astype(bf16)
        low = (rest - middle.astype(f32)).astype(bf16)
        terms = [contract(hot.astype(bf16), term, ((1,), (0,))) for term in (high, middle, low)]
        return terms[0] + (terms[1] + terms[2])

    pulsar_hot = onehot(pulsar_ref[...], pulsar_total)
    backend_hot = onehot(backend_ref[...], efac_ref.shape[1])

    def lookup(ref):
        columns = contract(ref[...], pulsar_hot, ((0,), (0,)), HIGH)
        return jnp.sum(columns * backend_hot, axis=0, keepdims=True)

    factor = lookup(efac_ref)
    floor_term = lookup(equad_ref)
    stacked = jnp.concatenate(
        [
            factor * factor,
            floor_term * floor_term,
            counts_ref[...].astype(f32),
            jnp.zeros((5, tile_total), f32),
        ],
        axis=0,
    )
    columns = jnp.transpose(stacked)
    lane = lax.broadcasted_iota(jnp.int32, (tile_total, row_total), 1).astype(f32)
    error = error_ref[...]
    weight = jnp.where(
        lane < columns[:, 2:3], 1.0 / (columns[:, 0:1] * (error * error) + columns[:, 1:2]), 0.0
    )
    weights[...] = weight

    slot = slot_ref[...]
    dest = slot // tile_total
    place = (slot - dest * tile_total).astype(f32)
    dest_hot = onehot(dest, peers)
    earlier = (
        lax.broadcasted_iota(jnp.int32, (tile_total, tile_total), 0)
        < lax.broadcasted_iota(jnp.int32, (tile_total, tile_total), 1)
    ).astype(f32)
    before = contract(dest_hot, earlier, ((1,), (0,)))
    rank = jnp.sum(before * dest_hot, axis=0, keepdims=True)
    position = lax.rem(dest - me + peers, peers) * per_peer + rank.astype(jnp.int32)
    order = onehot(position, tile_total)
    white = jnp.sqrt(weight) * residual_ref[...]
    ordered = exact(order, white).reshape(sorted_rows.shape)
    sorted_rows[...] = ordered
    got_rows[0] = ordered[0]
    places = contract(place, order, ((1,), (1,))).astype(jnp.int32)
    aim = lax.broadcasted_iota(jnp.int32, (peers, tile_total), 0)
    spot = lax.broadcasted_iota(jnp.int32, (peers, tile_total), 1)
    spread_places = jnp.where(spot // per_peer == aim, places, 0)
    sorted_places[...] = spread_places.reshape(sorted_places.shape)
    got_places[0] = spread_places[0:1]

    def remote(source, target, n, d):
        return pltpu.make_async_remote_copy(
            src_ref=source,
            dst_ref=target.at[d],
            send_sem=sends.at[n],
            recv_sem=arrivals.at[n],
            device_id={"toa": lax.rem(me + d, peers)},
            device_id_type=MESH,
        )

    def arrived(target, n):
        rest = target.at[pl.ds(1, peers - 1)]
        pltpu.make_async_copy(rest, rest, sends.at[n]).wait()
        pltpu.make_async_copy(rest, rest, arrivals.at[n]).wait()

    def send_rows(d):
        remote(sorted_rows.at[d], got_rows, ROWS, d).start()
        remote(sorted_places.at[d], got_places, PLACES, d).start()

    each(1, peers, send_rows)

    def spread(ref, g, wide):
        block = chunk(ref, g)[...].astype(f32)
        for c in range(cuts):
            cut = block[:, :, c * LANES : (c + 1) * LANES]
            for j in range(half):
                wide[c, j * PITCH : j * PITCH + group, :] = cut[j]

    def columns_of(wide, i):
        return jnp.concatenate(
            [wide[c, pl.ds(i, SPAN, stride=PITCH), :] for c in range(cuts)], axis=1
        )

    ends = half // 8 * 8
    below = lax.broadcasted_iota(jnp.int32, (stored - ends, row_total), 0) == half - ends
    nothing = jnp.zeros((SPAN - stored, row_total), f32)
    first_lanes = lax.broadcasted_iota(jnp.int32, (stored, LANES), 1) < SPAN

    def multiply(grams, pair, left, right):
        both = contract(
            jnp.concatenate(left, axis=0), jnp.concatenate(right, axis=0), ((1,), (1,))
        )
        first, step = pair
        row = pl.multiple_of(first * (group // 2 * apart), 8) + step * apart
        grams[pl.ds(row, stored), :] = jnp.where(
            first_lanes, both[:stored], both[SPAN : SPAN + stored]
        )

    def own_chunk(g, wide):
        start = pl.multiple_of(g * group, group)
        weight = weights[pl.ds(start, group), :]
        residual = residual_ref[pl.ds(start, group), :]
        for i in range(0, group, 2):
            left, right = [], []
            for k in (i, i + 1):
                basis = columns_of(wide, k)
                with_residual = jnp.where(below, residual[k : k + 1, :], basis[ends:stored])
                one = jnp.concatenate([basis[:ends], with_residual], axis=0)
                one = jnp.concatenate([weight[k : k + 1, :] * one, nothing], axis=0).astype(bf16)
                lefts[start + k] = one
                left.append(one)
                right.append(basis.astype(bf16))
            multiply(own_grams, (g, i // 2), left, right)

    def cross_chunk(g):
        swap(g).wait_recv()
        spread(other_store, g, wide_even)
        start = (core * swaps + g) * group
        for i in range(0, group, 2):
            left = [lefts[start + i], lefts[start + i + 1]]
            right = [columns_of(wide_even, k).astype(bf16) for k in (i, i + 1)]
            multiply(cross_grams, (g, i // 2), left, right)

    evens = lax.broadcasted_iota(jnp.int32, (tile_total, tile_total), 0)
    pairs = lax.broadcasted_iota(jnp.int32, (tile_total, tile_total), 1)
    count = tile_total // 2
    halves = jnp.where(pairs < count, 2 * pairs, 2 * (pairs - count) + 1)
    parted = contract(pulsar_hot, (evens == halves).astype(f32), ((1,), (0,))).astype(bf16)
    own_chosen = jnp.concatenate([parted[:, :count], parted[:, count:]], axis=0)
    cross_chosen = jnp.where(core == 0, own_chosen[:, : count // 2], own_chosen[:, count // 2 :])
    low_lanes = lax.broadcasted_iota(jnp.int32, (pulsar_total, LANES), 1) < SPAN

    def picked(grams, chosen, j):
        return grams[pl.ds(j, chosen.shape[1], stride=apart), :]

    def joined(out):
        return out[:pulsar_total], out[pulsar_total:]

    def gather(grams, chosen, target, last):
        for j in range(FOLD):
            sides = [picked(grams, chosen, i).astype(bf16) for i in (j, j + FOLD) if i < half]
            even, odd = joined(contract(chosen, jnp.concatenate(sides, axis=1), ((1,), (0,))))
            if len(sides) == 2:
                fixed = jnp.where(low_lanes, even[:, :LANES], odd[:, LANES:])
                moved = jnp.where(low_lanes, even[:, LANES:], odd[:, :LANES])
                value = fixed + pltpu.roll(moved, SPAN, 1)
            else:
                value = even + pltpu.roll(odd, SPAN, 1)
                value = jnp.where(low_lanes, value, last.get(j + FOLD, 0.0))
            part_wide[pl.ds(j, pulsar_total, stride=PART), :] = value
        for p in range(pulsar_total):
            target[p] = part_wide[p * PART : p * PART + FOLD, :].astype(bf16)

    def projections():
        terms = picked(own_grams, own_chosen, half)
        high = terms.astype(bf16)
        low = (terms - high.astype(f32)).astype(bf16)
        doubled = jnp.concatenate([own_chosen, own_chosen], axis=1)
        even, odd = joined(contract(doubled, jnp.concatenate([high, low], axis=0), ((1,), (0,))))
        value = odd + pltpu.roll(even, SPAN, 1)
        coarse = value.astype(bf16).astype(f32)
        return {half: coarse, half + 1: value - coarse}

    def send_part(part, target, n):
        def one(d):
            first = lax.rem(me + d, peers) * owned
            remote(part.at[pl.ds(first, owned)], target, n, d).start()

        each(1, peers, one)

    def total(part, target):
        mine = part[pl.ds(me * owned, owned)].astype(f32)
        return lax.fori_loop(1, peers, lambda d, acc: acc + target[d].astype(f32), mine)

    def own_chunks(h):
        load(2 * h + 1).wait()

        @pl.when(h < steps // 2 - 1)
        def _():
            load(2 * h + 2).wait()

        spread(own_store, 2 * h + 1, wide_odd)
        own_chunk(2 * h, wide_even)
        spread(own_store, jnp.minimum(2 * h + 2, steps - 1), wide_even)
        own_chunk(2 * h + 1, wide_odd)

    load(0).wait()
    spread(own_store, 0, wide_even)
    each(0, steps // 2, own_chunks)
    gather(own_grams, own_chosen, own_part, projections())
    send_part(own_part, got_own, OWN)
    each(0, swaps, cross_chunk)
    gather(cross_grams, cross_chosen, cross_part, {})
    send_part(cross_part, got_cross, CROSS)

    arrived(got_rows, ROWS)
    arrived(got_places, PLACES)
    home = onehot(jnp.sum(got_places[...], axis=0), tile_total)
    white_ref[...] = exact(home, got_rows[...].reshape(tile_total, row_total))
    everything = other_store
    pltpu.make_async_copy(everything, everything, sends.at[SWAP]).wait()
    arrived(got_own, OWN)
    own_sum = total(own_part, got_own)
    arrived(got_cross, CROSS)
    cross_sum[...] = total(cross_part, got_cross)
    last = pltpu.make_async_remote_copy(
        src_ref=cross_sum,
        dst_ref=partner_sum,
        send_sem=last_sems.at[0],
        recv_sem=last_sems.at[1],
        device_id={"rep": partner},
        device_id_type=MESH,
    )
    last.start()

    def unfold(block):
        return jnp.concatenate([block[:, :SPAN], block[:, SPAN:]], axis=0)

    for q in range(owned):
        block = unfold(own_sum[q])
        projection_ref[q : q + 1, :] = (
            block[half : half + 1, :half] + block[half + 1 : half + 2, :half]
        )
    last.wait()
    first_core = core == 0
    for q in range(owned):
        mine = unfold(own_sum[q])[:half, :half]
        turned = jnp.transpose(unfold(partner_sum[q]))
        theirs = unfold(cross_sum[q])[:half, :half] + turned[:half, :half]
        gram_ref[:, q, :half] = jnp.where(first_core, mine, theirs)
        gram_ref[:, q, half:] = jnp.where(first_core, theirs, mine)


def finish_kernel(gram_in, projection_in, white_in, gram_out, projection_out, white_out, sems):
    copies = [
        pltpu.make_async_copy(source, target, sems.at[n])
        for n, (source, target) in enumerate(
            [(white_in, white_out), (gram_in, gram_out), (projection_in, projection_out)]
        )
    ]
    for copy in copies:
        copy.start()
    for copy in copies:
        copy.wait()


def shards(
    residual, toa_error, basis_rows, efac_table, equad_table, pulsar, backend, counts, owner_slot
):
    tile_total, row_total = residual.shape
    peers = lax.axis_size("toa")
    half = basis_rows.shape[1]
    pulsar_total, backend_total = efac_table.shape
    owned = pulsar_total // peers
    per_peer = tile_total // peers
    group = min(GROUP, tile_total)
    steps = tile_total // group
    cuts = row_total // LANES
    stored = round_up(half + 1, 8)
    f32 = jnp.float32
    bf16 = jnp.bfloat16
    i32 = jnp.int32
    anywhere = pl.BlockSpec(memory_space=pltpu.HBM)
    vmem = pl.BlockSpec(memory_space=pltpu.VMEM)

    def row(vector):
        return vector.reshape(1, tile_total)

    results = [
        ((half, owned, 2 * half), f32),
        ((owned, half), f32),
        ((tile_total, row_total), f32),
    ]
    held = pl.pallas_call(
        functools.partial(whole_kernel, peers),
        in_specs=[anywhere] * 9,
        out_specs=[vmem] * 3,
        out_shape=[pltpu.VMEM(shape, dtype) for shape, dtype in results],
        scratch_shapes=[
            pltpu.VMEM((1, tile_total), i32),
            pltpu.VMEM((1, tile_total), i32),
            pltpu.VMEM((1, tile_total), i32),
            pltpu.VMEM((1, tile_total), i32),
            pltpu.VMEM((pulsar_total, backend_total), f32),
            pltpu.VMEM((pulsar_total, backend_total), f32),
            pltpu.VMEM((tile_total, row_total), f32),
            pltpu.VMEM((tile_total, row_total), f32),
            pltpu.VMEM((peers, per_peer, row_total), f32),
            pltpu.VMEM((peers, per_peer, row_total), f32),
            pltpu.VMEM((peers, 1, tile_total), i32),
            pltpu.VMEM((peers, 1, tile_total), i32),
            pltpu.VMEM((half, tile_total, row_total), bf16),
            pltpu.VMEM((half, tile_total // 2, row_total), bf16),
            pltpu.VMEM((tile_total, row_total), f32),
            pltpu.VMEM((cuts, SPAN * PITCH, LANES), f32),
            pltpu.VMEM((cuts, SPAN * PITCH, LANES), f32),
            pltpu.VMEM((tile_total, SPAN, row_total), bf16),
            pltpu.VMEM((tile_total // 2 * (stored + 1), LANES), f32),
            pltpu.VMEM((tile_total // 4 * (stored + 1), LANES), f32),
            pltpu.VMEM((pulsar_total * PART, LANES), f32),
            pltpu.VMEM((pulsar_total, FOLD, LANES), bf16),
            pltpu.VMEM((pulsar_total, FOLD, LANES), bf16),
            pltpu.VMEM((peers, owned, FOLD, LANES), bf16),
            pltpu.VMEM((peers, owned, FOLD, LANES), bf16),
            pltpu.VMEM((owned, FOLD, LANES), f32),
            pltpu.VMEM((owned, FOLD, LANES), f32),
            pltpu.SemaphoreType.DMA((8,)),
            pltpu.SemaphoreType.DMA((steps,)),
            pltpu.SemaphoreType.DMA((steps // 2,)),
            pltpu.SemaphoreType.DMA((5,)),
            pltpu.SemaphoreType.DMA((5,)),
            pltpu.SemaphoreType.DMA((2,)),
        ],
        compiler_params=pltpu.CompilerParams(
            collective_id=0, has_side_effects=True, vmem_limit_bytes=VMEM_KERNEL
        ),
        name="whole",
    )(
        *[
            pltpu.with_memory_space_constraint(value, pltpu.HBM)
            for value in (
                row(pulsar),
                row(backend),
                row(counts),
                row(owner_slot),
                efac_table,
                equad_table,
                residual,
                toa_error,
                jnp.transpose(basis_rows, (1, 0, 2)),
            )
        ]
    )
    gram, projection, whitened = pl.pallas_call(
        finish_kernel,
        in_specs=[vmem] * 3,
        out_specs=[anywhere] * 3,
        out_shape=[jax.ShapeDtypeStruct(shape, dtype) for shape, dtype in results],
        scratch_shapes=[pltpu.SemaphoreType.DMA((3,))],
        name="finish",
    )(*[pltpu.with_memory_space_constraint(value, pltpu.VMEM) for value in held])
    return (jnp.transpose(gram, (1, 2, 0)), projection, whitened)


def solution(mesh):
    in_specs = (
        P("toa", None),
        P("toa", None),
        P("toa", "rep", None),
        P(),
        P(),
        P("toa"),
        P("toa"),
        P("toa"),
        P("toa"),
    )
    out_specs = (P("toa", None, "rep"), P("toa", "rep"), P("toa", None))
    return jax.shard_map(shards, mesh=mesh, in_specs=in_specs, out_specs=out_specs, check_vma=False)
```

```python
import functools

import jax
import jax.numpy as jnp
from jax import lax
from jax.experimental import pallas as pl
from jax.experimental.pallas import tpu as pltpu
from jax.sharding import PartitionSpec as P

MESH = pl.DeviceIdType.MESH
GROUP = 16
LANES = 128
SPAN = LANES // 2
PITCH = GROUP + 1
SIDE = SPAN // 2
FOLD = SIDE // 2
VMEM_KERNEL = 48 * 1024 * 1024
HIGH = lax.Precision.HIGHEST
SWAP, ROWS, PLACES, OWN, CROSS, LAST = range(6)


def round_up(value, step):
    return (value + step - 1) // step * step


def contract(left, right, dims, precision=None):
    return lax.dot_general(
        left, right, (dims, ((), ())), precision=precision, preferred_element_type=jnp.float32
    )


def whole_kernel(
    peers,
    pulsar_hbm,
    backend_hbm,
    counts_hbm,
    slot_hbm,
    efac_hbm,
    equad_hbm,
    residual_hbm,
    error_hbm,
    basis_ref,
    gram_ref,
    projection_ref,
    white_ref,
    pulsar_ref,
    backend_ref,
    counts_ref,
    slot_ref,
    efac_ref,
    equad_ref,
    residual_ref,
    error_ref,
    sorted_rows,
    got_rows,
    sorted_places,
    got_places,
    own_store,
    other_store,
    weights,
    wide_even,
    wide_odd,
    lefts,
    own_grams,
    cross_grams,
    part_wide,
    own_part,
    cross_part,
    got_own,
    got_cross,
    cross_sum,
    partner_sum,
    own_square,
    small_sems,
    load_sems,
    swap_arrivals,
    sends,
    arrivals,
):
    me = lax.axis_index("toa")
    core = lax.axis_index("rep")
    partner = 1 - core
    half, tile_total, row_total = basis_ref.shape
    pulsar_total = efac_hbm.shape[0]
    owned = pulsar_total // peers
    per_peer = tile_total // peers
    group = min(GROUP, tile_total)
    steps = tile_total // group
    swaps = steps // 2
    cuts = row_total // LANES
    side = (half + 1) // 2
    stored = SPAN
    apart = stored + 1
    f32 = jnp.float32
    bf16 = jnp.bfloat16

    barrier = pltpu.get_barrier_semaphore()
    pl.semaphore_signal(barrier, inc=1, device_id={"rep": partner}, device_id_type=MESH)

    def each(first, last, action):
        def body(i, carry):
            action(i)
            return carry

        lax.fori_loop(first, last, body, 0)

    def greet(d):
        pl.semaphore_signal(
            barrier, inc=1, device_id={"toa": lax.rem(me + d, peers)}, device_id_type=MESH
        )


    small = [
        pltpu.make_async_copy(source, target, small_sems.at[n])
        for n, (source, target) in enumerate(
            [
                (pulsar_hbm, pulsar_ref),
                (backend_hbm, backend_ref),
                (efac_hbm, efac_ref),
                (equad_hbm, equad_ref),
                (counts_hbm, counts_ref),
                (slot_hbm, slot_ref),
                (error_hbm, error_ref),
                (residual_hbm, residual_ref),
            ]
        )
    ]
    for copy in small:
        copy.start()

    def chunk(ref, g):
        return ref.at[:, pl.ds(pl.multiple_of(g * group, group), group), :]

    def load(g):
        return pltpu.make_async_copy(chunk(basis_ref, g), chunk(own_store, g), load_sems.at[g])

    each(0, steps, lambda g: load(g).start())
    each(1, peers, greet)

    def swap(g):
        return pltpu.make_async_remote_copy(
            src_ref=chunk(basis_ref, partner * swaps + g),
            dst_ref=chunk(other_store, g),
            send_sem=sends.at[SWAP],
            recv_sem=swap_arrivals.at[g],
            device_id={"rep": partner},
            device_id_type=MESH,
        )


    for wide in (wide_even, wide_odd):
        for c in range(cuts):
            for first, last in ((side, SIDE), (SIDE + half - side, SPAN)):
                blank = jnp.zeros(((last - first) * PITCH, LANES), f32)
                wide[c, first * PITCH : last * PITCH, :] = blank
    for copy in small:
        copy.wait()

    def onehot(row, amount):
        index = lax.broadcasted_iota(jnp.int32, (amount, row.shape[1]), 0)
        return (index == row).astype(f32)

    pulsar_hot = onehot(pulsar_ref[...], pulsar_total)
    backend_hot = onehot(backend_ref[...], efac_ref.shape[1])

    def lookup(ref):
        columns = contract(ref[...], pulsar_hot, ((0,), (0,)), HIGH)
        return jnp.sum(columns * backend_hot, axis=0, keepdims=True)

    factor = lookup(efac_ref)
    floor_term = lookup(equad_ref)
    stacked = jnp.concatenate(
        [
            factor * factor,
            floor_term * floor_term,
            counts_ref[...].astype(f32),
            jnp.zeros((5, tile_total), f32),
        ],
        axis=0,
    )
    columns = jnp.transpose(stacked)
    lane = lax.broadcasted_iota(jnp.int32, (tile_total, row_total), 1).astype(f32)
    error = error_ref[...]
    weight = jnp.where(
        lane < columns[:, 2:3], 1.0 / (columns[:, 0:1] * (error * error) + columns[:, 1:2]), 0.0
    )
    weights[...] = weight

    slot = slot_ref[...]
    dest = slot // tile_total
    place = (slot - dest * tile_total).astype(f32)
    dest_hot = onehot(dest, peers)
    earlier = (
        lax.broadcasted_iota(jnp.int32, (tile_total, tile_total), 0)
        < lax.broadcasted_iota(jnp.int32, (tile_total, tile_total), 1)
    ).astype(f32)
    before = contract(dest_hot, earlier, ((1,), (0,)))
    rank = jnp.sum(before * dest_hot, axis=0, keepdims=True)
    position = lax.rem(dest - me + peers, peers) * per_peer + rank.astype(jnp.int32)
    order = onehot(position, tile_total)
    white = jnp.sqrt(weight) * residual_ref[...]
    ordered = contract(order.astype(bf16), white.astype(bf16), ((1,), (0,)))
    ordered = ordered.reshape(peers, per_peer, row_total)
    pieces = [ordered[:, :, c * LANES : (c + 1) * LANES] for c in range(cuts)]
    unused = sorted_rows.shape[1] - cuts * per_peer
    if unused:
        pieces.append(jnp.zeros((peers, unused, LANES), f32))
    message = jnp.concatenate(pieces, axis=1).astype(bf16)
    sorted_rows[...] = message
    got_rows[0] = message[0]
    places = contract(place, order, ((1,), (1,))).astype(jnp.int32)
    aim = lax.broadcasted_iota(jnp.int32, (peers, tile_total), 0)
    spot = lax.broadcasted_iota(jnp.int32, (peers, tile_total), 1)
    spread_places = jnp.where(spot // per_peer == aim, places, 0)
    sorted_places[...] = spread_places.reshape(sorted_places.shape)
    got_places[0] = spread_places[0:1]

    def remote(source, target, n, d):
        return pltpu.make_async_remote_copy(
            src_ref=source,
            dst_ref=target.at[d],
            send_sem=sends.at[n],
            recv_sem=arrivals.at[n],
            device_id={"toa": lax.rem(me + d, peers)},
            device_id_type=MESH,
        )

    def arrived(target, n):
        rest = target.at[pl.ds(1, peers - 1)]
        pltpu.make_async_copy(rest, rest, sends.at[n]).wait()
        pltpu.make_async_copy(rest, rest, arrivals.at[n]).wait()

    def send_rows(d):
        remote(sorted_rows.at[d], got_rows, ROWS, d).start()
        remote(sorted_places.at[d], got_places, PLACES, d).start()


    def spread(ref, g, wide, piece=0, pieces=1):
        start = pl.multiple_of(g * group, group)
        for j in range(half * piece // pieces, half * (piece + 1) // pieces):
            block = ref[j, pl.ds(start, group), :].astype(f32)
            at = (j if j < side else j - side + SIDE) * PITCH
            for c in range(cuts):
                wide[c, at : at + group, :] = block[:, c * LANES : (c + 1) * LANES]

    def columns_of(wide, i):
        return jnp.concatenate(
            [wide[c, pl.ds(i, SPAN, stride=PITCH), :] for c in range(cuts)], axis=1
        )

    starts = side // 8 * 8
    below = lax.broadcasted_iota(jnp.int32, (8, row_total), 0) == side - starts
    first_lanes = lax.broadcasted_iota(jnp.int32, (stored, LANES), 1) < SPAN

    def multiply(grams, pair, left, right):
        both = contract(
            jnp.concatenate(left, axis=0), jnp.concatenate(right, axis=0), ((1,), (1,))
        )
        first, step = pair
        row = pl.multiple_of(first * (group // 2 * apart), 8) + step * apart
        grams[pl.ds(row, stored), :] = jnp.where(
            first_lanes, both[:stored], both[SPAN : SPAN + stored]
        )

    def own_chunk(g, wide, later, other):
        start = pl.multiple_of(g * group, group)
        weight = weights[pl.ds(start, group), :]
        residual = residual_ref[pl.ds(start, group), :]
        for i in range(0, group, 2):
            spread(own_store, later, other, i // 2, group // 2)
            left, right = [], []
            for k in (i, i + 1):
                basis = columns_of(wide, k)
                around = basis[starts : starts + 8]
                around = jnp.where(below, residual[k : k + 1, :], around)
                one = jnp.concatenate([basis[:starts], around, basis[starts + 8 :]], axis=0)
                one = (weight[k : k + 1, :] * one).astype(bf16)
                lefts[start + k] = one
                left.append(one)
                right.append(basis.astype(bf16))
            multiply(own_grams, (g, i // 2), left, right)

    def cross_chunk(g):
        swap(g).wait_recv()
        spread(other_store, g, wide_even)
        start = (core * swaps + g) * group
        for i in range(0, group, 2):
            mine = [lefts[start + i], lefts[start + i + 1]]
            theirs = [columns_of(wide_even, k).astype(bf16) for k in (i, i + 1)]
            left = [jnp.where(core == 0, a, b) for a, b in zip(mine, theirs)]
            right = [jnp.where(core == 0, b, a) for a, b in zip(mine, theirs)]
            multiply(cross_grams, (g, i // 2), left, right)

    evens = lax.broadcasted_iota(jnp.int32, (tile_total, tile_total), 0)
    pairs = lax.broadcasted_iota(jnp.int32, (tile_total, tile_total), 1)
    count = tile_total // 2
    halves = jnp.where(pairs < count, 2 * pairs, 2 * (pairs - count) + 1)
    parted = contract(pulsar_hot, (evens == halves).astype(f32), ((1,), (0,))).astype(bf16)
    own_chosen = jnp.concatenate([parted[:, :count], parted[:, count:]], axis=0)
    cross_chosen = jnp.where(core == 0, own_chosen[:, : count // 2], own_chosen[:, count // 2 :])
    low_lanes = lax.broadcasted_iota(jnp.int32, (pulsar_total, LANES), 1) < SPAN

    def picked(grams, chosen, j):
        return grams[pl.ds(j, chosen.shape[1], stride=apart), :]

    def joined(out):
        return out[:pulsar_total], out[pulsar_total:]

    lanes = lax.broadcasted_iota(jnp.int32, (pulsar_total, LANES), 1)
    inner = lax.rem(lanes, SPAN)

    apart_part = SIDE + 1

    def summed(grams, chosen, slots):
        sides = [picked(grams, chosen, slot).astype(bf16) for slot in slots]
        even, odd = joined(contract(chosen, jnp.concatenate(sides, axis=1), ((1,), (0,))))
        return [
            jnp.where(low_lanes, even[:, at : at + LANES], odd[:, at : at + LANES])
            for at in range(0, len(slots) * LANES, LANES)
        ]

    def fold(low, high):
        moved = jnp.where(low_lanes, high, low)
        return jnp.where(low_lanes, low, high) + pltpu.roll(moved, SPAN, 1)

    def put(row, value):
        part_wide[pl.ds(row, pulsar_total, stride=apart_part), :] = value

    def settle(target):
        count = target.shape[1]
        for p in range(pulsar_total):
            target[p] = part_wide[p * apart_part : p * apart_part + count, :].astype(bf16)

    zero = jnp.zeros((pulsar_total, LANES), f32)

    def gather_own():
        diagonal = zero
        merged = []
        for j in range(side):
            if j >= half - side:
                merged.append(summed(own_grams, own_chosen, (j,))[0])
                continue
            first, second = summed(own_grams, own_chosen, (j, SIDE + j))
            diagonal = diagonal + jnp.where(inner == SIDE + j, second, 0.0)
            second = pltpu.roll(second, LANES - SIDE, 1)
            merged.append(jnp.where((inner > j) & (inner < SIDE), second, first))
            if j >= FOLD:
                put(j - FOLD, fold(merged[j - FOLD], merged[j]))
        coarse, fine = projections()
        extra = [diagonal, coarse, fine]
        for j in range(side, SIDE):
            high = extra[j - side] if j - side < len(extra) else zero
            put(j - FOLD, fold(merged[j - FOLD], high))
        settle(own_part)

    def gather_cross():
        for h in range(2):
            most = side if h == 0 else half - side
            for r in range(FOLD):
                slots = [SIDE * h + j for j in (r, r + FOLD) if j < most]
                found = summed(cross_grams, cross_chosen, slots) + [zero] * (2 - len(slots))
                put(h * FOLD + r, fold(found[0], found[1]))
        settle(cross_part)

    def projections():
        terms = picked(own_grams, own_chosen, side)
        high = terms.astype(bf16)
        low = (terms - high.astype(f32)).astype(bf16)
        doubled = jnp.concatenate([own_chosen, own_chosen], axis=1)
        even, odd = joined(contract(doubled, jnp.concatenate([high, low], axis=0), ((1,), (0,))))
        terms = jnp.where(low_lanes, even, odd)
        value = terms + pltpu.roll(terms, SPAN, 1)
        coarse = value.astype(bf16).astype(f32)
        alone = [jnp.where(low_lanes, term, 0.0) for term in (coarse, value - coarse)]
        return alone

    def send_part(part, target, n):
        def one(d):
            first = lax.rem(me + d, peers) * owned
            remote(part.at[pl.ds(first, owned)], target, n, d).start()

        each(1, peers, one)

    def total(part, target):
        mine = part[pl.ds(me * owned, owned)].astype(f32)
        return lax.fori_loop(1, peers, lambda d, acc: acc + target[d].astype(f32), mine)

    def own_chunks(h):
        load(2 * h + 1).wait()

        @pl.when(h < steps // 2 - 1)
        def _():
            load(2 * h + 2).wait()

        own_chunk(2 * h, wide_even, 2 * h + 1, wide_odd)
        own_chunk(2 * h + 1, wide_odd, jnp.minimum(2 * h + 2, steps - 1), wide_even)

    load(0).wait()
    spread(own_store, 0, wide_even)
    each(0, steps // 4, own_chunks)
    pl.semaphore_wait(barrier, peers)
    each(0, swaps, lambda g: swap(g).start())
    each(1, peers, send_rows)
    each(steps // 4, steps // 2, own_chunks)
    gather_own()
    send_part(own_part, got_own, OWN)
    each(0, swaps, cross_chunk)
    gather_cross()

    def to_partner(source, target, n):
        return pltpu.make_async_remote_copy(
            src_ref=source,
            dst_ref=target,
            send_sem=sends.at[n],
            recv_sem=arrivals.at[n],
            device_id={"rep": partner},
            device_id_type=MESH,
        )

    send_part(cross_part, got_cross, CROSS)

    arrived(got_rows, ROWS)
    arrived(got_places, PLACES)
    home = onehot(jnp.sum(got_places[...], axis=0), tile_total)
    messages = got_rows[...].astype(f32)
    for c in range(cuts):
        rows = messages[:, c * per_peer : (c + 1) * per_peer, :].reshape(tile_total, LANES)
        white_ref[:, c * LANES : (c + 1) * LANES] = contract(
            home.astype(bf16), rows.astype(bf16), ((1,), (0,))
        )
    everything = other_store
    pltpu.make_async_copy(everything, everything, sends.at[SWAP]).wait()
    arrived(got_own, OWN)
    own_sum = total(own_part, got_own)
    row_at = lax.broadcasted_iota(jnp.int32, (SIDE, SIDE), 0)
    lane_at = lax.broadcasted_iota(jnp.int32, (SIDE, SIDE), 1)
    place_at = lax.broadcasted_iota(jnp.int32, (SPAN, LANES), 1)
    rest = half - side

    def unfold(block):
        return jnp.concatenate([block[:, :SPAN], block[:, SPAN:]], axis=0)

    def compact(square):
        square = jnp.concatenate([square, jnp.zeros((square.shape[0], SPAN), f32)], axis=1)
        return jnp.where(place_at < side, square, pltpu.roll(square, LANES - SIDE + side, 1))

    for q in range(owned):
        rows = unfold(own_sum[q])
        merged, mixed = rows[:, :SIDE], rows[:, SIDE:]
        turned = jnp.transpose(merged)
        diagonal = rows[side : side + 1, SIDE:]
        upper = jnp.where(lane_at < row_at, turned, diagonal)
        upper = jnp.where(lane_at > row_at, merged, upper)
        lower = jnp.where(lane_at <= row_at, merged, turned)
        square = jnp.concatenate(
            [
                jnp.concatenate([lower, mixed], axis=1),
                jnp.concatenate([jnp.transpose(mixed), upper], axis=1),
            ],
            axis=0,
        )
        square = compact(square)
        own_square[q] = jnp.where(core == 0, square, pltpu.roll(square, half, 1))
        found = rows[side + 1 : side + 2] + rows[side + 2 : side + 3]
        projection_ref[q : q + 1, :side] = found[:, :side]
        projection_ref[q : q + 1, side:] = found[:, SIDE : SIDE + rest]
    arrived(got_cross, CROSS)
    cross_sum[...] = total(cross_part, got_cross)
    last = to_partner(cross_sum, partner_sum, LAST)
    last.start()
    last.wait()
    for q in range(owned):
        both = cross_sum[q] + partner_sum[q]
        both = jnp.concatenate([unfold(both[:FOLD]), unfold(both[FOLD:])], axis=0)
        both = compact(jnp.where(core == 0, both, jnp.transpose(both)))
        both = jnp.where(core == 0, pltpu.roll(both, half, 1), both)
        mine = (place_at < half) == (core == 0)
        whole = jnp.where(mine, own_square[q], both)
        gram_ref[:side, q, :] = whole[:side, : 2 * half]
        gram_ref[side:, q, :] = whole[SIDE : SIDE + rest, : 2 * half]


def finish_kernel(gram_in, projection_in, white_in, gram_out, projection_out, white_out, sems):
    copies = [
        pltpu.make_async_copy(source, target, sems.at[n])
        for n, (source, target) in enumerate(
            [(white_in, white_out), (gram_in, gram_out), (projection_in, projection_out)]
        )
    ]
    for copy in copies:
        copy.start()
    for copy in copies:
        copy.wait()


def shards(
    residual, toa_error, basis_rows, efac_table, equad_table, pulsar, backend, counts, owner_slot
):
    tile_total, row_total = residual.shape
    peers = lax.axis_size("toa")
    half = basis_rows.shape[1]
    pulsar_total, backend_total = efac_table.shape
    owned = pulsar_total // peers
    per_peer = tile_total // peers
    group = min(GROUP, tile_total)
    steps = tile_total // group
    cuts = row_total // LANES
    message = round_up(cuts * per_peer, 16)
    f32 = jnp.float32
    bf16 = jnp.bfloat16
    i32 = jnp.int32
    anywhere = pl.BlockSpec(memory_space=pltpu.HBM)
    vmem = pl.BlockSpec(memory_space=pltpu.VMEM)

    def row(vector):
        return vector.reshape(1, tile_total)

    results = [
        ((half, owned, 2 * half), f32),
        ((owned, half), f32),
        ((tile_total, row_total), f32),
    ]
    held = pl.pallas_call(
        functools.partial(whole_kernel, peers),
        in_specs=[anywhere] * 9,
        out_specs=[vmem] * 3,
        out_shape=[pltpu.VMEM(shape, dtype) for shape, dtype in results],
        scratch_shapes=[
            pltpu.VMEM((1, tile_total), i32),
            pltpu.VMEM((1, tile_total), i32),
            pltpu.VMEM((1, tile_total), i32),
            pltpu.VMEM((1, tile_total), i32),
            pltpu.VMEM((pulsar_total, backend_total), f32),
            pltpu.VMEM((pulsar_total, backend_total), f32),
            pltpu.VMEM((tile_total, row_total), f32),
            pltpu.VMEM((tile_total, row_total), f32),
            pltpu.VMEM((peers, message, LANES), bf16),
            pltpu.VMEM((peers, message, LANES), bf16),
            pltpu.VMEM((peers, 1, tile_total), i32),
            pltpu.VMEM((peers, 1, tile_total), i32),
            pltpu.VMEM((half, tile_total, row_total), bf16),
            pltpu.VMEM((half, tile_total // 2, row_total), bf16),
            pltpu.VMEM((tile_total, row_total), f32),
            pltpu.VMEM((cuts, SPAN * PITCH, LANES), f32),
            pltpu.VMEM((cuts, SPAN * PITCH, LANES), f32),
            pltpu.VMEM((tile_total, SPAN, row_total), bf16),
            pltpu.VMEM((tile_total // 2 * (SPAN + 1), LANES), f32),
            pltpu.VMEM((tile_total // 4 * (SPAN + 1), LANES), f32),
            pltpu.VMEM((pulsar_total * (SIDE + 1), LANES), f32),
            pltpu.VMEM((pulsar_total, FOLD, LANES), bf16),
            pltpu.VMEM((pulsar_total, SIDE, LANES), bf16),
            pltpu.VMEM((peers, owned, FOLD, LANES), bf16),
            pltpu.VMEM((peers, owned, SIDE, LANES), bf16),
            pltpu.VMEM((owned, SIDE, LANES), f32),
            pltpu.VMEM((owned, SIDE, LANES), f32),
            pltpu.VMEM((owned, SPAN, LANES), f32),
            pltpu.SemaphoreType.DMA((8,)),
            pltpu.SemaphoreType.DMA((steps,)),
            pltpu.SemaphoreType.DMA((steps // 2,)),
            pltpu.SemaphoreType.DMA((6,)),
            pltpu.SemaphoreType.DMA((6,)),
        ],
        compiler_params=pltpu.CompilerParams(
            collective_id=0, has_side_effects=True, vmem_limit_bytes=VMEM_KERNEL
        ),
        name="whole",
    )(
        *[
            pltpu.with_memory_space_constraint(value, pltpu.HBM)
            for value in (
                row(pulsar),
                row(backend),
                row(counts),
                row(owner_slot),
                efac_table,
                equad_table,
                residual,
                toa_error,
                jnp.transpose(basis_rows, (1, 0, 2)),
            )
        ]
    )
    gram, projection, whitened = pl.pallas_call(
        finish_kernel,
        in_specs=[vmem] * 3,
        out_specs=[anywhere] * 3,
        out_shape=[jax.ShapeDtypeStruct(shape, dtype) for shape, dtype in results],
        scratch_shapes=[pltpu.SemaphoreType.DMA((3,))],
        name="finish",
    )(*[pltpu.with_memory_space_constraint(value, pltpu.VMEM) for value in held])
    return (jnp.transpose(gram, (1, 2, 0)), projection, whitened)


def solution(mesh):
    in_specs = (
        P("toa", None),
        P("toa", None),
        P("toa", "rep", None),
        P(),
        P(),
        P("toa"),
        P("toa"),
        P("toa"),
        P("toa"),
    )
    out_specs = (P("toa", None, "rep"), P("toa", "rep"), P("toa", None))
    return jax.shard_map(shards, mesh=mesh, in_specs=in_specs, out_specs=out_specs, check_vma=False)
```

```python
import functools

import jax
import jax.numpy as jnp
from jax import lax
from jax.experimental import pallas as pl
from jax.experimental.pallas import tpu as pltpu
from jax.sharding import PartitionSpec as P

MESH = pl.DeviceIdType.MESH
GROUP = 16
LANES = 128
PITCH = GROUP + 1
SHORT = 16
TALL = 32
VMEM_KERNEL = 48 * 1024 * 1024
HIGH = lax.Precision.HIGHEST
SWAP, ROWS, OWN, CROSS, LAST = range(5)


def round_up(value, step):
    return (value + step - 1) // step * step


def contract(left, right, dims, precision=None):
    return lax.dot_general(
        left, right, (dims, ((), ())), precision=precision, preferred_element_type=jnp.float32
    )


def whole_kernel(
    peers,
    pulsar_hbm,
    backend_hbm,
    counts_hbm,
    slot_hbm,
    efac_hbm,
    equad_hbm,
    residual_hbm,
    error_hbm,
    basis_ref,
    gram_ref,
    projection_ref,
    white_ref,
    pulsar_ref,
    backend_ref,
    counts_ref,
    slot_ref,
    efac_ref,
    equad_ref,
    residual_ref,
    error_ref,
    sorted_rows,
    got_rows,
    places_ref,
    own_store,
    other_store,
    weights,
    wide_even,
    wide_odd,
    lefts,
    own_grams,
    cross_grams,
    part_wide,
    own_part,
    cross_part,
    got_own,
    got_cross,
    cross_sum,
    partner_sum,
    own_square,
    small_sems,
    load_sems,
    swap_arrivals,
    sends,
    arrivals,
):
    me = lax.axis_index("toa")
    core = lax.axis_index("rep")
    partner = 1 - core
    half, tile_total, row_total = basis_ref.shape
    pulsar_total = efac_hbm.shape[0]
    owned = pulsar_total // peers
    per_peer = tile_total // peers
    group = min(GROUP, tile_total)
    steps = tile_total // group
    swaps = steps // 2
    cuts = row_total // LANES
    side = (half + 1) // 2
    quarter = (side + 1) // 2
    span = round_up(half + 1, 8)
    apart = span + 1
    apart_part = TALL + 1
    f32 = jnp.float32
    bf16 = jnp.bfloat16

    barrier = pltpu.get_barrier_semaphore()
    pl.semaphore_signal(barrier, inc=1, device_id={"rep": partner}, device_id_type=MESH)

    def each(first, last, action):
        def body(i, carry):
            action(i)
            return carry

        lax.fori_loop(first, last, body, 0)

    def greet(d):
        pl.semaphore_signal(
            barrier, inc=1, device_id={"toa": lax.rem(me + d, peers)}, device_id_type=MESH
        )


    small = [
        pltpu.make_async_copy(source, target, small_sems.at[n])
        for n, (source, target) in enumerate(
            [
                (pulsar_hbm, pulsar_ref),
                (backend_hbm, backend_ref),
                (efac_hbm, efac_ref),
                (equad_hbm, equad_ref),
                (counts_hbm, counts_ref),
                (slot_hbm, slot_ref),
                (error_hbm, error_ref),
                (residual_hbm, residual_ref),
            ]
        )
    ]
    for copy in small:
        copy.start()

    def chunk(ref, g):
        return ref.at[:, pl.ds(pl.multiple_of(g * group, group), group), :]

    def load(g):
        return pltpu.make_async_copy(chunk(basis_ref, g), chunk(own_store, g), load_sems.at[g])

    def turn(p):
        return lax.rem(partner * swaps + p, steps)

    each(0, steps, lambda p: load(turn(p)).start())
    each(1, peers, greet)

    def swap(g):
        return pltpu.make_async_remote_copy(
            src_ref=chunk(basis_ref, partner * swaps + g),
            dst_ref=chunk(other_store, g),
            send_sem=sends.at[SWAP],
            recv_sem=swap_arrivals.at[g],
            device_id={"rep": partner},
            device_id_type=MESH,
        )


    for wide in (wide_even, wide_odd):
        for c in range(cuts):
            wide[c, half * PITCH :, :] = jnp.zeros(((span - half) * PITCH, LANES), f32)
    for copy in small:
        copy.wait()

    def onehot(row, amount):
        index = lax.broadcasted_iota(jnp.int32, (amount, row.shape[1]), 0)
        return (index == row).astype(f32)

    pulsar_hot = onehot(pulsar_ref[...], pulsar_total)
    backend_hot = onehot(backend_ref[...], efac_ref.shape[1])

    def lookup(ref):
        columns = contract(ref[...], pulsar_hot, ((0,), (0,)), HIGH)
        return jnp.sum(columns * backend_hot, axis=0, keepdims=True)

    factor = lookup(efac_ref)
    floor_term = lookup(equad_ref)
    stacked = jnp.concatenate(
        [
            factor * factor,
            floor_term * floor_term,
            counts_ref[...].astype(f32),
            jnp.zeros((5, tile_total), f32),
        ],
        axis=0,
    )
    columns = jnp.transpose(stacked)
    lane = lax.broadcasted_iota(jnp.int32, (tile_total, row_total), 1).astype(f32)
    error = error_ref[...]
    weight = jnp.where(
        lane < columns[:, 2:3], 1.0 / (columns[:, 0:1] * (error * error) + columns[:, 1:2]), 0.0
    )
    weights[...] = weight

    slot = slot_ref[...]
    dest = slot // tile_total
    place = (slot - dest * tile_total).astype(f32)
    dest_hot = onehot(dest, peers)
    earlier = (
        lax.broadcasted_iota(jnp.int32, (tile_total, tile_total), 0)
        < lax.broadcasted_iota(jnp.int32, (tile_total, tile_total), 1)
    ).astype(f32)
    before = contract(dest_hot, earlier, ((1,), (0,)))
    rank = jnp.sum(before * dest_hot, axis=0, keepdims=True)
    position = lax.rem(dest - me + peers, peers) * per_peer + rank.astype(jnp.int32)
    order = onehot(position, tile_total)
    white = jnp.sqrt(weight) * residual_ref[...]
    ordered = contract(order.astype(bf16), white.astype(bf16), ((1,), (0,)))
    ordered = ordered.reshape(peers, per_peer, row_total)
    pieces = [ordered[:, :, c * LANES : (c + 1) * LANES] for c in range(cuts)]
    unused = sorted_rows.shape[1] - cuts * per_peer
    if unused:
        pieces.append(jnp.zeros((peers, unused, LANES), f32))
    message = jnp.concatenate(pieces, axis=1).astype(bf16)
    sorted_rows[...] = message
    got_rows[0] = message[0]
    places = contract(dest_hot * place, order, ((1,), (1,)))
    places_ref[...] = jnp.repeat(places, owned, axis=0) if owned > 1 else places

    def remote(source, target, n, d):
        return pltpu.make_async_remote_copy(
            src_ref=source,
            dst_ref=target.at[d],
            send_sem=sends.at[n],
            recv_sem=arrivals.at[n],
            device_id={"toa": lax.rem(me + d, peers)},
            device_id_type=MESH,
        )

    def arrived(target, n):
        rest = target.at[pl.ds(1, peers - 1)]
        pltpu.make_async_copy(rest, rest, sends.at[n]).wait()
        pltpu.make_async_copy(rest, rest, arrivals.at[n]).wait()

    def send_rows(d):
        remote(sorted_rows.at[d], got_rows, ROWS, d).start()


    def spread(ref, g, wide, piece=0, pieces=1):
        start = pl.multiple_of(g * group, group)
        for j in range(half * piece // pieces, half * (piece + 1) // pieces):
            block = ref[j, pl.ds(start, group), :].astype(f32)
            at = j * PITCH
            for c in range(cuts):
                wide[c, at : at + group, :] = block[:, c * LANES : (c + 1) * LANES]

    def columns_of(wide, i):
        return jnp.concatenate(
            [wide[c, pl.ds(i, span, stride=PITCH), :] for c in range(cuts)], axis=1
        )

    starts = half // 8 * 8
    below = lax.broadcasted_iota(jnp.int32, (span - starts, row_total), 0) == half - starts
    first_lanes = lax.broadcasted_iota(jnp.int32, (span, 2 * span), 1) < span
    unused_lanes = jnp.zeros((span, LANES - 2 * span), f32)

    def multiply(grams, g, step, left, right):
        both = contract(left, right, ((1,), (1,)))
        both = jnp.where(first_lanes, both[:span], both[span:])
        row = pl.multiple_of(g * (group // 2 * apart), 8) + step * apart
        grams[pl.ds(row, span), :] = jnp.concatenate([both, unused_lanes], axis=1)

    def own_chunk(p, wide, other, keep):
        g = turn(p)
        later = turn(jnp.minimum(p + 1, steps - 1))
        start = pl.multiple_of(g * group, group)
        weight = weights[pl.ds(start, group), :]
        residual = residual_ref[pl.ds(start, group), :]
        spread(own_store, later, other)
        for i in range(0, group, 2):
            bases = [columns_of(wide, k) for k in (i, i + 1)]
            scaled = []
            for k, basis in zip((i, i + 1), bases):
                with_residual = jnp.where(below, residual[k : k + 1, :], basis[starts:])
                one = jnp.concatenate([basis[:starts], with_residual], axis=0)
                scaled.append(weight[k : k + 1, :] * one)
            left = jnp.concatenate(scaled, axis=0).astype(bf16)
            if keep:
                lefts[(p - swaps) * (group // 2) + i // 2] = left
            right = jnp.concatenate(bases, axis=0).astype(bf16)
            multiply(own_grams, g, i // 2, left, right)

    def cross_chunk(g):
        swap(g).wait_recv()
        spread(other_store, g, wide_even)
        for i in range(0, group, 2):
            bases = [columns_of(wide_even, k) for k in (i, i + 1)]
            right = jnp.concatenate(bases, axis=0).astype(bf16)
            multiply(cross_grams, g, i // 2, lefts[g * (group // 2) + i // 2], right)

    evens = lax.broadcasted_iota(jnp.int32, (tile_total, tile_total), 0)
    pairs = lax.broadcasted_iota(jnp.int32, (tile_total, tile_total), 1)
    count = tile_total // 2
    halves = jnp.where(pairs < count, 2 * pairs, 2 * (pairs - count) + 1)
    parted = contract(pulsar_hot, (evens == halves).astype(f32), ((1,), (0,))).astype(bf16)
    own_chosen = jnp.concatenate([parted[:, :count], parted[:, count:]], axis=0)
    cross_chosen = jnp.where(core == 0, own_chosen[:, : count // 2], own_chosen[:, count // 2 :])
    lanes = lax.broadcasted_iota(jnp.int32, (pulsar_total, LANES), 1)
    low_lanes = lanes < span
    inner = jnp.where(low_lanes, lanes, lanes - span)

    def picked(grams, chosen, j):
        return grams[pl.ds(j, chosen.shape[1], stride=apart), :]

    def joined(out):
        return out[:pulsar_total], out[pulsar_total:]

    def summed(grams, chosen, slots):
        sides = [picked(grams, chosen, slot).astype(bf16) for slot in slots]
        even, odd = joined(contract(chosen, jnp.concatenate(sides, axis=1), ((1,), (0,))))
        return [
            jnp.where(low_lanes, even[:, at : at + LANES], odd[:, at : at + LANES])
            for at in range(0, len(slots) * LANES, LANES)
        ]

    def fold(low, high):
        low = low + pltpu.roll(low, LANES - span, 1)
        high = high + pltpu.roll(high, span, 1)
        return jnp.where(low_lanes, low, high)

    def put(row, value):
        part_wide[pl.ds(row, pulsar_total, stride=apart_part), :] = value

    def settle(target):
        count = target.shape[1]
        for p in range(pulsar_total):
            target[p] = part_wide[p * apart_part : p * apart_part + count, :].astype(bf16)

    zero = jnp.zeros((pulsar_total, LANES), f32)

    def gather_own():
        diagonal = zero
        merged = []
        for j in range(side):
            if j >= half - side:
                merged.append(summed(own_grams, own_chosen, (j,))[0])
            else:
                first, second = summed(own_grams, own_chosen, (j, side + j))
                diagonal = diagonal + jnp.where(inner == side + j, second, 0.0)
                second = pltpu.roll(second, LANES - side, 1)
                merged.append(jnp.where((inner > j) & (inner < side), second, first))
        for j in range(quarter - 1):
            put(j, fold(merged[j], merged[j + quarter]))
        put(quarter - 1, fold(merged[quarter - 1], diagonal))
        put(quarter, projections())
        for row in range(quarter + 1, SHORT - 1):
            put(row, zero)
        put(SHORT - 1, places_ref[...])
        settle(own_part)

    def gather_cross():
        for r in range(TALL):
            slots = [j for j in (r, r + TALL) if j < half]
            found = summed(cross_grams, cross_chosen, slots) + [zero] * (2 - len(slots))
            put(r, fold(found[0], found[1]))
        settle(cross_part)

    def projections():
        terms = picked(own_grams, own_chosen, half)
        high = terms.astype(bf16)
        low = (terms - high.astype(f32)).astype(bf16)
        doubled = jnp.concatenate([own_chosen, own_chosen], axis=1)
        even, odd = joined(contract(doubled, jnp.concatenate([high, low], axis=0), ((1,), (0,))))
        value = fold(jnp.where(low_lanes, even, odd), zero)
        coarse = value.astype(bf16).astype(f32)
        return jnp.where(low_lanes, coarse, pltpu.roll(value - coarse, span, 1))

    def send_part(part, target, n):
        def one(d):
            first = lax.rem(me + d, peers) * owned
            remote(part.at[pl.ds(first, owned)], target, n, d).start()

        each(1, peers, one)

    def total(part, target):
        mine = part[pl.ds(me * owned, owned)].astype(f32)
        return lax.fori_loop(1, peers, lambda d, acc: acc + target[d].astype(f32), mine)

    def own_chunks(keep, h):
        load(turn(2 * h + 1)).wait()

        @pl.when(h < steps // 2 - 1)
        def _():
            load(turn(2 * h + 2)).wait()

        own_chunk(2 * h, wide_even, wide_odd, keep)
        own_chunk(2 * h + 1, wide_odd, wide_even, keep)

    load(turn(0)).wait()
    spread(own_store, turn(0), wide_even)
    pl.semaphore_wait(barrier, peers)
    each(0, swaps, lambda g: swap(g).start())
    each(1, peers, send_rows)
    each(0, steps // 4, functools.partial(own_chunks, False))
    each(steps // 4, steps // 2, functools.partial(own_chunks, True))
    gather_own()
    send_part(own_part, got_own, OWN)
    each(0, swaps, cross_chunk)
    gather_cross()
    send_part(cross_part, got_cross, CROSS)

    def to_partner(source, target, n):
        return pltpu.make_async_remote_copy(
            src_ref=source,
            dst_ref=target,
            send_sem=sends.at[n],
            recv_sem=arrivals.at[n],
            device_id={"rep": partner},
            device_id_type=MESH,
        )

    arrived(got_cross, CROSS)
    cross_sum[...] = total(cross_part, got_cross)
    last = to_partner(cross_sum, partner_sum, LAST)
    last.start()
    everything = other_store
    pltpu.make_async_copy(everything, everything, sends.at[SWAP]).wait()
    arrived(got_rows, ROWS)
    arrived(got_own, OWN)
    own_sum = total(own_part, got_own)
    home = onehot(own_sum[0][SHORT - 1 : SHORT].astype(jnp.int32), tile_total)
    messages = got_rows[...].astype(f32)
    for c in range(cuts):
        rows = messages[:, c * per_peer : (c + 1) * per_peer, :].reshape(tile_total, LANES)
        white_ref[:, c * LANES : (c + 1) * LANES] = contract(
            home.astype(bf16), rows.astype(bf16), ((1,), (0,))
        )
    row_at = lax.broadcasted_iota(jnp.int32, (TALL, TALL), 0)
    lane_at = lax.broadcasted_iota(jnp.int32, (TALL, TALL), 1)
    place_at = lax.broadcasted_iota(jnp.int32, (span, LANES), 1)
    rest = half - side

    for q in range(owned):
        block = own_sum[q]
        high = pltpu.roll(block, LANES - span, 1)
        rows = [block[:quarter], high[: side - quarter], jnp.zeros((TALL - side, LANES), f32)]
        rows = jnp.concatenate(rows, axis=0)
        merged = rows[:, :TALL]
        mixed = rows[:, side : side + TALL]
        turned = jnp.transpose(merged)
        diagonal = high[quarter - 1 : quarter, side : side + TALL]
        upper = jnp.where(lane_at < row_at, turned, diagonal)
        upper = jnp.where(lane_at > row_at, merged, upper)
        lower = jnp.where(lane_at <= row_at, merged, turned)
        own_square[q, :side, :side] = lower[:side, :side]
        own_square[q, :side, side:half] = mixed[:side, :rest]
        own_square[q, side:half, :side] = jnp.transpose(mixed)[:rest, :side]
        own_square[q, side:half, side:half] = upper[:rest, :rest]
        square = own_square[q]
        own_square[q] = jnp.where(core == 0, square, pltpu.roll(square, half, 1))
        found = block[quarter : quarter + 1] + high[quarter : quarter + 1]
        projection_ref[q : q + 1, :] = found[:, :half]

    def unfold(block):
        return jnp.concatenate([block[:, :span], block[: span - TALL, span : 2 * span]], axis=0)

    last.wait()
    for q in range(owned):
        both = unfold(cross_sum[q]) + jnp.transpose(unfold(partner_sum[q]))
        both = jnp.concatenate([both, jnp.zeros((span, LANES - span), f32)], axis=1)
        both = jnp.where(core == 0, pltpu.roll(both, half, 1), both)
        mine = (place_at < half) == (core == 0)
        gram_ref[:, q, :] = jnp.where(mine, own_square[q], both)[:half, : 2 * half]


def finish_kernel(gram_in, projection_in, white_in, gram_out, projection_out, white_out, sems):
    copies = [
        pltpu.make_async_copy(source, target, sems.at[n])
        for n, (source, target) in enumerate(
            [(white_in, white_out), (gram_in, gram_out), (projection_in, projection_out)]
        )
    ]
    for copy in copies:
        copy.start()
    for copy in copies:
        copy.wait()


def shards(
    residual, toa_error, basis_rows, efac_table, equad_table, pulsar, backend, counts, owner_slot
):
    tile_total, row_total = residual.shape
    peers = lax.axis_size("toa")
    half = basis_rows.shape[1]
    pulsar_total, backend_total = efac_table.shape
    owned = pulsar_total // peers
    per_peer = tile_total // peers
    group = min(GROUP, tile_total)
    steps = tile_total // group
    cuts = row_total // LANES
    span = round_up(half + 1, 8)
    message = round_up(cuts * per_peer, 16)
    f32 = jnp.float32
    bf16 = jnp.bfloat16
    i32 = jnp.int32
    anywhere = pl.BlockSpec(memory_space=pltpu.HBM)
    vmem = pl.BlockSpec(memory_space=pltpu.VMEM)

    def row(vector):
        return vector.reshape(1, tile_total)

    results = [
        ((half, owned, 2 * half), f32),
        ((owned, half), f32),
        ((tile_total, row_total), f32),
    ]
    held = pl.pallas_call(
        functools.partial(whole_kernel, peers),
        in_specs=[anywhere] * 9,
        out_specs=[vmem] * 3,
        out_shape=[pltpu.VMEM(shape, dtype) for shape, dtype in results],
        scratch_shapes=[
            pltpu.VMEM((1, tile_total), i32),
            pltpu.VMEM((1, tile_total), i32),
            pltpu.VMEM((1, tile_total), i32),
            pltpu.VMEM((1, tile_total), i32),
            pltpu.VMEM((pulsar_total, backend_total), f32),
            pltpu.VMEM((pulsar_total, backend_total), f32),
            pltpu.VMEM((tile_total, row_total), f32),
            pltpu.VMEM((tile_total, row_total), f32),
            pltpu.VMEM((peers, message, LANES), bf16),
            pltpu.VMEM((peers, message, LANES), bf16),
            pltpu.VMEM((pulsar_total, tile_total), f32),
            pltpu.VMEM((half, tile_total, row_total), bf16),
            pltpu.VMEM((half, tile_total // 2, row_total), bf16),
            pltpu.VMEM((tile_total, row_total), f32),
            pltpu.VMEM((cuts, span * PITCH, LANES), f32),
            pltpu.VMEM((cuts, span * PITCH, LANES), f32),
            pltpu.VMEM((tile_total // 4, 2 * span, row_total), bf16),
            pltpu.VMEM((tile_total // 2 * (span + 1), LANES), f32),
            pltpu.VMEM((tile_total // 4 * (span + 1), LANES), f32),
            pltpu.VMEM((pulsar_total * (TALL + 1), LANES), f32),
            pltpu.VMEM((pulsar_total, SHORT, LANES), bf16),
            pltpu.VMEM((pulsar_total, TALL, LANES), bf16),
            pltpu.VMEM((peers, owned, SHORT, LANES), bf16),
            pltpu.VMEM((peers, owned, TALL, LANES), bf16),
            pltpu.VMEM((owned, TALL, LANES), f32),
            pltpu.VMEM((owned, TALL, LANES), f32),
            pltpu.VMEM((owned, span, LANES), f32),
            pltpu.SemaphoreType.DMA((8,)),
            pltpu.SemaphoreType.DMA((steps,)),
            pltpu.SemaphoreType.DMA((steps // 2,)),
            pltpu.SemaphoreType.DMA((5,)),
            pltpu.SemaphoreType.DMA((5,)),
        ],
        compiler_params=pltpu.CompilerParams(
            collective_id=0, has_side_effects=True, vmem_limit_bytes=VMEM_KERNEL
        ),
        name="whole",
    )(
        *[
            pltpu.with_memory_space_constraint(value, pltpu.HBM)
            for value in (
                row(pulsar),
                row(backend),
                row(counts),
                row(owner_slot),
                efac_table,
                equad_table,
                residual,
                toa_error,
                jnp.transpose(basis_rows, (1, 0, 2)),
            )
        ]
    )
    gram, projection, whitened = pl.pallas_call(
        finish_kernel,
        in_specs=[vmem] * 3,
        out_specs=[anywhere] * 3,
        out_shape=[jax.ShapeDtypeStruct(shape, dtype) for shape, dtype in results],
        scratch_shapes=[pltpu.SemaphoreType.DMA((3,))],
        name="finish",
    )(*[pltpu.with_memory_space_constraint(value, pltpu.VMEM) for value in held])
    return (jnp.transpose(gram, (1, 2, 0)), projection, whitened)


def solution(mesh):
    in_specs = (
        P("toa", None),
        P("toa", None),
        P("toa", "rep", None),
        P(),
        P(),
        P("toa"),
        P("toa"),
        P("toa"),
        P("toa"),
    )
    out_specs = (P("toa", None, "rep"), P("toa", "rep"), P("toa", None))
    return jax.shard_map(shards, mesh=mesh, in_specs=in_specs, out_specs=out_specs, check_vma=False)
```

```python
import functools

import jax
import jax.numpy as jnp
from jax import lax
from jax.experimental import pallas as pl
from jax.experimental.pallas import tpu as pltpu
from jax.sharding import PartitionSpec as P

MESH = pl.DeviceIdType.MESH
GROUP = 16
BURST = 15
LANES = 128
PITCH = GROUP + 1
SHORT = 16
TALL = 32
VMEM_KERNEL = 48 * 1024 * 1024
SWAP, ROWS, OWN, CROSS, LAST = range(5)


def round_up(value, step):
    return (value + step - 1) // step * step


def contract(left, right, dims):
    return lax.dot_general(
        left, right, (dims, ((), ())), preferred_element_type=jnp.float32
    )


def whole_kernel(
    peers,
    pulsar_hbm,
    backend_hbm,
    counts_hbm,
    slot_hbm,
    efac_hbm,
    equad_hbm,
    residual_hbm,
    error_hbm,
    basis_ref,
    gram_ref,
    projection_ref,
    white_ref,
    pulsar_ref,
    backend_ref,
    counts_ref,
    slot_ref,
    efac_ref,
    equad_ref,
    residual_ref,
    error_ref,
    sorted_rows,
    got_rows,
    places_ref,
    own_store,
    other_store,
    weights,
    wide_even,
    wide_odd,
    lefts,
    own_grams,
    cross_grams,
    part_wide,
    own_part,
    cross_part,
    got_own,
    got_cross,
    cross_sum,
    partner_sum,
    own_square,
    small_sems,
    load_sems,
    swap_arrivals,
    sends,
    arrivals,
):
    me = lax.axis_index("toa")
    core = lax.axis_index("rep")
    partner = 1 - core
    half, tile_total, row_total = basis_ref.shape
    pulsar_total = efac_hbm.shape[0]
    owned = pulsar_total // peers
    per_peer = tile_total // peers
    group = min(GROUP, tile_total)
    steps = tile_total // group
    swaps = steps // 2
    cuts = row_total // LANES
    side = (half + 1) // 2
    quarter = (side + 1) // 2
    span = round_up(half + 1, 8)
    apart = span + 1
    apart_part = TALL + 1
    f32 = jnp.float32
    bf16 = jnp.bfloat16

    barrier = pltpu.get_barrier_semaphore()
    pl.semaphore_signal(barrier, inc=1, device_id={"rep": partner}, device_id_type=MESH)

    def each(first, last, action):
        def body(i, carry):
            action(i)
            return carry

        lax.fori_loop(first, last, body, 0)

    def each_peer(action):
        step = BURST if (peers - 1) % BURST == 0 else 1

        def burst(i):
            for k in range(step):
                action(1 + i * step + k)

        each(0, (peers - 1) // step, burst)

    def greet(d):
        pl.semaphore_signal(
            barrier, inc=1, device_id={"toa": lax.rem(me + d, peers)}, device_id_type=MESH
        )


    small = [
        pltpu.make_async_copy(source, target, small_sems.at[n])
        for n, (source, target) in enumerate(
            [
                (pulsar_hbm, pulsar_ref),
                (backend_hbm, backend_ref),
                (efac_hbm, efac_ref),
                (equad_hbm, equad_ref),
                (counts_hbm, counts_ref),
                (slot_hbm, slot_ref),
                (error_hbm, error_ref),
                (residual_hbm, residual_ref),
            ]
        )
    ]
    for copy in small:
        copy.start()
    each_peer(greet)

    def chunk(ref, g):
        return ref.at[:, pl.ds(pl.multiple_of(g * group, group), group), :]

    def load(g):
        return pltpu.make_async_copy(chunk(basis_ref, g), chunk(own_store, g), load_sems.at[g])

    def turn(p):
        return lax.rem(partner * swaps + p, steps)

    each(0, steps, lambda p: load(turn(p)).start())

    def swap(g):
        return pltpu.make_async_remote_copy(
            src_ref=chunk(basis_ref, partner * swaps + g),
            dst_ref=chunk(other_store, g),
            send_sem=sends.at[SWAP],
            recv_sem=swap_arrivals.at[g],
            device_id={"rep": partner},
            device_id_type=MESH,
        )


    for wide in (wide_even, wide_odd):
        for c in range(cuts):
            wide[c, half * PITCH :, :] = jnp.zeros(((span - half) * PITCH, LANES), f32)
    for copy in small:
        copy.wait()

    def onehot(row, amount):
        index = lax.broadcasted_iota(jnp.int32, (amount, row.shape[1]), 0)
        return (index == row).astype(f32)

    pulsar_hot = onehot(pulsar_ref[...], pulsar_total)
    backend_hot = onehot(backend_ref[...], efac_ref.shape[1])

    def terms_of(values):
        high = values.astype(bf16)
        rest = values - high.astype(f32)
        middle = rest.astype(bf16)
        return [high, middle, (rest - middle.astype(f32)).astype(bf16)]

    def lookup(ref):
        table = jnp.concatenate(terms_of(ref[...]), axis=0)
        hot = jnp.concatenate([pulsar_hot.astype(bf16)] * 3, axis=0)
        columns = contract(table, hot, ((0,), (0,)))
        return jnp.sum(columns * backend_hot, axis=0, keepdims=True)

    factor = lookup(efac_ref)
    floor_term = lookup(equad_ref)
    stacked = jnp.concatenate(
        [
            factor * factor,
            floor_term * floor_term,
            counts_ref[...].astype(f32),
            jnp.zeros((5, tile_total), f32),
        ],
        axis=0,
    )
    columns = jnp.transpose(stacked)
    lane = lax.broadcasted_iota(jnp.int32, (tile_total, row_total), 1).astype(f32)
    error = error_ref[...]
    weight = jnp.where(
        lane < columns[:, 2:3], 1.0 / (columns[:, 0:1] * (error * error) + columns[:, 1:2]), 0.0
    )
    weights[...] = weight

    slot = slot_ref[...]
    dest = slot // tile_total
    place = (slot - dest * tile_total).astype(f32)
    dest_hot = onehot(dest, peers)
    earlier = (
        lax.broadcasted_iota(jnp.int32, (tile_total, tile_total), 0)
        < lax.broadcasted_iota(jnp.int32, (tile_total, tile_total), 1)
    ).astype(bf16)
    before = contract(dest_hot.astype(bf16), earlier, ((1,), (0,)))
    rank = jnp.sum(before * dest_hot, axis=0, keepdims=True)
    position = lax.rem(dest - me + peers, peers) * per_peer + rank.astype(jnp.int32)
    order = onehot(position, tile_total).astype(bf16)
    white = jnp.sqrt(weight) * residual_ref[...]
    ordered = contract(order, white.astype(bf16), ((1,), (0,)))
    ordered = ordered.reshape(peers, per_peer, row_total)
    pieces = [ordered[:, :, c * LANES : (c + 1) * LANES] for c in range(cuts)]
    unused = sorted_rows.shape[1] - cuts * per_peer
    if unused:
        pieces.append(jnp.zeros((peers, unused, LANES), f32))
    message = jnp.concatenate(pieces, axis=1).astype(bf16)
    sorted_rows[...] = message
    got_rows[0] = message[0]
    places = contract((dest_hot * place).astype(bf16), order, ((1,), (1,)))
    places_ref[...] = jnp.repeat(places, owned, axis=0) if owned > 1 else places

    def remote(source, target, n, d):
        return pltpu.make_async_remote_copy(
            src_ref=source,
            dst_ref=target.at[d],
            send_sem=sends.at[n],
            recv_sem=arrivals.at[n],
            device_id={"toa": lax.rem(me + d, peers)},
            device_id_type=MESH,
        )

    def arrived(target, n):
        rest = target.at[pl.ds(1, peers - 1)]
        pltpu.make_async_copy(rest, rest, arrivals.at[n]).wait()

    def gone(target, n):
        rest = target.at[pl.ds(1, peers - 1)]
        pltpu.make_async_copy(rest, rest, sends.at[n]).wait()

    def send_rows(d):
        remote(sorted_rows.at[d], got_rows, ROWS, d).start()


    def spread(ref, g, wide, piece=0, pieces=1):
        start = pl.multiple_of(g * group, group)
        for j in range(half * piece // pieces, half * (piece + 1) // pieces):
            block = ref[j, pl.ds(start, group), :].astype(f32)
            at = j * PITCH
            for c in range(cuts):
                wide[c, at : at + group, :] = block[:, c * LANES : (c + 1) * LANES]

    def columns_of(wide, i):
        return jnp.concatenate(
            [wide[c, pl.ds(i, span, stride=PITCH), :] for c in range(cuts)], axis=1
        )

    starts = half // 8 * 8
    below = lax.broadcasted_iota(jnp.int32, (span - starts, row_total), 0) == half - starts
    first_lanes = lax.broadcasted_iota(jnp.int32, (span, 2 * span), 1) < span
    unused_lanes = jnp.zeros((span, LANES - 2 * span), f32)

    def multiply(grams, g, step, left, right):
        both = contract(left, right, ((1,), (1,)))
        both = jnp.where(first_lanes, both[:span], both[span:])
        row = pl.multiple_of(g * (group // 2 * apart), 8) + step * apart
        grams[pl.ds(row, span), :] = jnp.concatenate([both, unused_lanes], axis=1)

    def own_chunk(p, wide, other, keep):
        g = turn(p)
        later = turn(jnp.minimum(p + 1, steps - 1))
        start = pl.multiple_of(g * group, group)
        weight = weights[pl.ds(start, group), :]
        residual = residual_ref[pl.ds(start, group), :]
        spread(own_store, later, other)
        for i in range(0, group, 2):
            bases = [columns_of(wide, k) for k in (i, i + 1)]
            scaled = []
            for k, basis in zip((i, i + 1), bases):
                with_residual = jnp.where(below, residual[k : k + 1, :], basis[starts:])
                one = jnp.concatenate([basis[:starts], with_residual], axis=0)
                scaled.append(weight[k : k + 1, :] * one)
            left = jnp.concatenate(scaled, axis=0).astype(bf16)
            if keep:
                lefts[(p - swaps) * (group // 2) + i // 2] = left
            right = jnp.concatenate(bases, axis=0).astype(bf16)
            multiply(own_grams, g, i // 2, left, right)

    def cross_chunk(g):
        spread(other_store, g, wide_even)
        for i in range(0, group, 2):
            bases = [columns_of(wide_even, k) for k in (i, i + 1)]
            right = jnp.concatenate(bases, axis=0).astype(bf16)
            multiply(cross_grams, g, i // 2, lefts[g * (group // 2) + i // 2], right)

    evens = lax.broadcasted_iota(jnp.int32, (tile_total, tile_total), 0)
    pairs = lax.broadcasted_iota(jnp.int32, (tile_total, tile_total), 1)
    count = tile_total // 2
    halves = jnp.where(pairs < count, 2 * pairs, 2 * (pairs - count) + 1)
    parted = contract(pulsar_hot.astype(bf16), (evens == halves).astype(bf16), ((1,), (0,)))
    parted = parted.astype(bf16)
    own_chosen = jnp.concatenate([parted[:, :count], parted[:, count:]], axis=0)
    cross_chosen = jnp.where(core == 0, own_chosen[:, : count // 2], own_chosen[:, count // 2 :])
    lanes = lax.broadcasted_iota(jnp.int32, (pulsar_total, LANES), 1)
    low_lanes = lanes < span
    inner = jnp.where(low_lanes, lanes, lanes - span)

    def picked(grams, chosen, j):
        return grams[pl.ds(j, chosen.shape[1], stride=apart), :]

    def joined(out):
        return out[:pulsar_total], out[pulsar_total:]

    def summed(grams, chosen, slots):
        sides = [picked(grams, chosen, slot).astype(bf16) for slot in slots]
        even, odd = joined(contract(chosen, jnp.concatenate(sides, axis=1), ((1,), (0,))))
        return [
            jnp.where(low_lanes, even[:, at : at + LANES], odd[:, at : at + LANES])
            for at in range(0, len(slots) * LANES, LANES)
        ]

    def fold(low, high):
        low = low + pltpu.roll(low, LANES - span, 1)
        high = high + pltpu.roll(high, span, 1)
        return jnp.where(low_lanes, low, high)

    def put(row, value):
        part_wide[pl.ds(row, pulsar_total, stride=apart_part), :] = value

    def settle(target):
        count = target.shape[1]
        for p in range(pulsar_total):
            target[p] = part_wide[p * apart_part : p * apart_part + count, :].astype(bf16)

    zero = jnp.zeros((pulsar_total, LANES), f32)

    def gather_own():
        diagonal = zero
        merged = []
        for j in range(side):
            if j >= half - side:
                merged.append(summed(own_grams, own_chosen, (j,))[0])
            else:
                first, second = summed(own_grams, own_chosen, (j, side + j))
                diagonal = diagonal + jnp.where(inner == side + j, second, 0.0)
                second = pltpu.roll(second, LANES - side, 1)
                merged.append(jnp.where((inner > j) & (inner < side), second, first))
        for j in range(quarter - 1):
            put(j, fold(merged[j], merged[j + quarter]))
        put(quarter - 1, fold(merged[quarter - 1], diagonal))
        put(quarter, projections())
        for row in range(quarter + 1, SHORT - 1):
            put(row, zero)
        put(SHORT - 1, places_ref[...])
        settle(own_part)

    def gather_cross():
        for r in range(side):
            slots = [j for j in (r, r + side) if j < half]
            found = summed(cross_grams, cross_chosen, slots) + [zero] * (2 - len(slots))
            put(r, fold(found[0], found[1]))
        for r in range(side, TALL):
            put(r, zero)
        settle(cross_part)

    def projections():
        terms = picked(own_grams, own_chosen, half)
        high = terms.astype(bf16)
        low = (terms - high.astype(f32)).astype(bf16)
        doubled = jnp.concatenate([own_chosen, own_chosen], axis=1)
        even, odd = joined(contract(doubled, jnp.concatenate([high, low], axis=0), ((1,), (0,))))
        value = fold(jnp.where(low_lanes, even, odd), zero)
        coarse = value.astype(bf16).astype(f32)
        return jnp.where(low_lanes, coarse, pltpu.roll(value - coarse, span, 1))

    def send_part(part, target, n):
        def one(d):
            first = lax.rem(me + d, peers) * owned
            remote(part.at[pl.ds(first, owned)], target, n, d).start()

        each_peer(one)

    def total(part, target):
        mine = part[pl.ds(me * owned, owned)].astype(f32)
        return mine + jnp.sum(target[pl.ds(1, peers - 1)].astype(f32), axis=0)

    def own_chunks(keep, h):
        load(turn(2 * h + 1)).wait()

        @pl.when(h < steps // 2 - 1)
        def _():
            load(turn(2 * h + 2)).wait()

        own_chunk(2 * h, wide_even, wide_odd, keep)
        own_chunk(2 * h + 1, wide_odd, wide_even, keep)

    load(turn(0)).wait()
    spread(own_store, turn(0), wide_even)
    pl.semaphore_wait(barrier, peers)
    each(0, swaps, lambda g: swap(g).start())
    each_peer(send_rows)
    each(0, steps // 4, functools.partial(own_chunks, False))
    each(steps // 4, steps // 2, functools.partial(own_chunks, True))
    swap(0).wait_recv()
    gather_own()
    cross_chunk(0)
    send_part(own_part, got_own, OWN)

    for g in range(1, swaps):
        swap(g).wait_recv()
        cross_chunk(g)
    gather_cross()
    send_part(cross_part, got_cross, CROSS)

    def to_partner(source, target, n):
        return pltpu.make_async_remote_copy(
            src_ref=source,
            dst_ref=target,
            send_sem=sends.at[n],
            recv_sem=arrivals.at[n],
            device_id={"rep": partner},
            device_id_type=MESH,
        )

    arrived(got_cross, CROSS)
    cross_sum[...] = total(cross_part, got_cross)
    last = to_partner(cross_sum, partner_sum, LAST)
    last.start()
    everything = other_store
    pltpu.make_async_copy(everything, everything, sends.at[SWAP]).wait()
    arrived(got_rows, ROWS)
    arrived(got_own, OWN)
    own_sum = total(own_part, got_own)
    home = onehot(own_sum[0][SHORT - 1 : SHORT].astype(jnp.int32), tile_total)
    messages = got_rows[...].astype(f32)
    for c in range(cuts):
        rows = messages[:, c * per_peer : (c + 1) * per_peer, :].reshape(tile_total, LANES)
        white_ref[:, c * LANES : (c + 1) * LANES] = contract(
            home.astype(bf16), rows.astype(bf16), ((1,), (0,))
        )
    row_at = lax.broadcasted_iota(jnp.int32, (TALL, TALL), 0)
    lane_at = lax.broadcasted_iota(jnp.int32, (TALL, TALL), 1)
    place_at = lax.broadcasted_iota(jnp.int32, (span, LANES), 1)
    rest = half - side

    for q in range(owned):
        block = own_sum[q]
        high = pltpu.roll(block, LANES - span, 1)
        rows = [block[:quarter], high[: side - quarter], jnp.zeros((TALL - side, LANES), f32)]
        rows = jnp.concatenate(rows, axis=0)
        merged = rows[:, :TALL]
        mixed = rows[:, side : side + TALL]
        turned = jnp.transpose(merged)
        diagonal = high[quarter - 1 : quarter, side : side + TALL]
        upper = jnp.where(lane_at < row_at, turned, diagonal)
        upper = jnp.where(lane_at > row_at, merged, upper)
        lower = jnp.where(lane_at <= row_at, merged, turned)
        own_square[q, :side, :side] = lower[:side, :side]
        own_square[q, :side, side:half] = mixed[:side, :rest]
        own_square[q, side:half, :side] = jnp.transpose(mixed)[:rest, :side]
        own_square[q, side:half, side:half] = upper[:rest, :rest]
        square = own_square[q]
        own_square[q] = jnp.where(core == 0, square, pltpu.roll(square, half, 1))
        found = block[quarter : quarter + 1] + high[quarter : quarter + 1]
        projection_ref[q : q + 1, :] = found[:, :half]

    def unfold(block):
        tall = [block[:side, :span], block[:rest, span : 2 * span]]
        return jnp.concatenate(tall + [jnp.zeros((span - half, span), f32)], axis=0)

    for target, n in ((got_rows, ROWS), (got_own, OWN), (got_cross, CROSS)):
        gone(target, n)
    last.wait()
    for q in range(owned):
        both = unfold(cross_sum[q]) + jnp.transpose(unfold(partner_sum[q]))
        both = jnp.concatenate([both, jnp.zeros((span, LANES - span), f32)], axis=1)
        both = jnp.where(core == 0, pltpu.roll(both, half, 1), both)
        mine = (place_at < half) == (core == 0)
        gram_ref[:, q, :] = jnp.where(mine, own_square[q], both)[:half, : 2 * half]


def finish_kernel(gram_in, projection_in, white_in, gram_out, projection_out, white_out, sems):
    copies = [
        pltpu.make_async_copy(source, target, sems.at[n])
        for n, (source, target) in enumerate(
            [(white_in, white_out), (gram_in, gram_out), (projection_in, projection_out)]
        )
    ]
    for copy in copies:
        copy.start()
    for copy in copies:
        copy.wait()


def shards(
    residual, toa_error, basis_rows, efac_table, equad_table, pulsar, backend, counts, owner_slot
):
    tile_total, row_total = residual.shape
    peers = lax.axis_size("toa")
    half = basis_rows.shape[1]
    pulsar_total, backend_total = efac_table.shape
    owned = pulsar_total // peers
    per_peer = tile_total // peers
    group = min(GROUP, tile_total)
    steps = tile_total // group
    cuts = row_total // LANES
    span = round_up(half + 1, 8)
    message = round_up(cuts * per_peer, 16)
    f32 = jnp.float32
    bf16 = jnp.bfloat16
    i32 = jnp.int32
    anywhere = pl.BlockSpec(memory_space=pltpu.HBM)
    vmem = pl.BlockSpec(memory_space=pltpu.VMEM)

    def row(vector):
        return vector.reshape(1, tile_total)

    results = [
        ((half, owned, 2 * half), f32),
        ((owned, half), f32),
        ((tile_total, row_total), f32),
    ]
    held = pl.pallas_call(
        functools.partial(whole_kernel, peers),
        in_specs=[anywhere] * 9,
        out_specs=[vmem] * 3,
        out_shape=[pltpu.VMEM(shape, dtype) for shape, dtype in results],
        scratch_shapes=[
            pltpu.VMEM((1, tile_total), i32),
            pltpu.VMEM((1, tile_total), i32),
            pltpu.VMEM((1, tile_total), i32),
            pltpu.VMEM((1, tile_total), i32),
            pltpu.VMEM((pulsar_total, backend_total), f32),
            pltpu.VMEM((pulsar_total, backend_total), f32),
            pltpu.VMEM((tile_total, row_total), f32),
            pltpu.VMEM((tile_total, row_total), f32),
            pltpu.VMEM((peers, message, LANES), bf16),
            pltpu.VMEM((peers, message, LANES), bf16),
            pltpu.VMEM((pulsar_total, tile_total), f32),
            pltpu.VMEM((half, tile_total, row_total), bf16),
            pltpu.VMEM((half, tile_total // 2, row_total), bf16),
            pltpu.VMEM((tile_total, row_total), f32),
            pltpu.VMEM((cuts, span * PITCH, LANES), f32),
            pltpu.VMEM((cuts, span * PITCH, LANES), f32),
            pltpu.VMEM((tile_total // 4, 2 * span, row_total), bf16),
            pltpu.VMEM((tile_total // 2 * (span + 1), LANES), f32),
            pltpu.VMEM((tile_total // 4 * (span + 1), LANES), f32),
            pltpu.VMEM((pulsar_total * (TALL + 1), LANES), f32),
            pltpu.VMEM((pulsar_total, SHORT, LANES), bf16),
            pltpu.VMEM((pulsar_total, TALL, LANES), bf16),
            pltpu.VMEM((peers, owned, SHORT, LANES), bf16),
            pltpu.VMEM((peers, owned, TALL, LANES), bf16),
            pltpu.VMEM((owned, TALL, LANES), f32),
            pltpu.VMEM((owned, TALL, LANES), f32),
            pltpu.VMEM((owned, span, LANES), f32),
            pltpu.SemaphoreType.DMA((8,)),
            pltpu.SemaphoreType.DMA((steps,)),
            pltpu.SemaphoreType.DMA((steps // 2,)),
            pltpu.SemaphoreType.DMA((5,)),
            pltpu.SemaphoreType.DMA((5,)),
        ],
        compiler_params=pltpu.CompilerParams(
            collective_id=0, has_side_effects=True, vmem_limit_bytes=VMEM_KERNEL
        ),
        name="whole",
    )(
        *[
            pltpu.with_memory_space_constraint(value, pltpu.HBM)
            for value in (
                row(pulsar),
                row(backend),
                row(counts),
                row(owner_slot),
                efac_table,
                equad_table,
                residual,
                toa_error,
                jnp.transpose(basis_rows, (1, 0, 2)),
            )
        ]
    )
    gram, projection, whitened = pl.pallas_call(
        finish_kernel,
        in_specs=[vmem] * 3,
        out_specs=[anywhere] * 3,
        out_shape=[jax.ShapeDtypeStruct(shape, dtype) for shape, dtype in results],
        scratch_shapes=[pltpu.SemaphoreType.DMA((3,))],
        name="finish",
    )(*[pltpu.with_memory_space_constraint(value, pltpu.VMEM) for value in held])
    return (jnp.transpose(gram, (1, 2, 0)), projection, whitened)


def solution(mesh):
    in_specs = (
        P("toa", None),
        P("toa", None),
        P("toa", "rep", None),
        P(),
        P(),
        P("toa"),
        P("toa"),
        P("toa"),
        P("toa"),
    )
    out_specs = (P("toa", None, "rep"), P("toa", "rep"), P("toa", None))
    return jax.shard_map(shards, mesh=mesh, in_specs=in_specs, out_specs=out_specs, check_vma=False)
```

```python
import functools

import jax
import jax.numpy as jnp
from jax import lax
from jax.experimental import pallas as pl
from jax.experimental.pallas import tpu as pltpu
from jax.sharding import PartitionSpec as P

MESH = pl.DeviceIdType.MESH
GROUP = 16
BURST = 15
LANES = 128
PITCH = GROUP + 1
SHORT = 16
TALL = 32
VMEM_KERNEL = 48 * 1024 * 1024
SWAP, ROWS, OWN, CROSS, LAST = range(5)


def round_up(value, step):
    return (value + step - 1) // step * step


def contract(left, right, dims):
    return lax.dot_general(
        left, right, (dims, ((), ())), preferred_element_type=jnp.float32
    )


def whole_kernel(
    peers,
    pulsar_hbm,
    backend_hbm,
    counts_hbm,
    slot_hbm,
    efac_hbm,
    equad_hbm,
    residual_hbm,
    error_hbm,
    basis_ref,
    gram_ref,
    projection_ref,
    white_ref,
    pulsar_ref,
    backend_ref,
    counts_ref,
    slot_ref,
    efac_ref,
    equad_ref,
    residual_ref,
    error_ref,
    sorted_rows,
    got_rows,
    places_ref,
    own_store,
    other_store,
    weights,
    wide_even,
    wide_odd,
    lefts,
    own_grams,
    cross_grams,
    part_wide,
    own_part,
    cross_part,
    got_own,
    got_cross,
    cross_sum,
    partner_sum,
    own_square,
    small_sems,
    load_sems,
    swap_arrivals,
    sends,
    arrivals,
):
    me = lax.axis_index("toa")
    core = lax.axis_index("rep")
    partner = 1 - core
    half, tile_total, row_total = basis_ref.shape
    pulsar_total = efac_hbm.shape[0]
    owned = pulsar_total // peers
    per_peer = tile_total // peers
    group = min(GROUP, tile_total)
    steps = tile_total // group
    swaps = steps // 2
    cuts = row_total // LANES
    side = (half + 1) // 2
    quarter = (side + 1) // 2
    span = round_up(half + 1, 8)
    apart = span + 1
    apart_part = TALL + 1
    f32 = jnp.float32
    bf16 = jnp.bfloat16

    barrier = pltpu.get_barrier_semaphore()
    pl.semaphore_signal(barrier, inc=1, device_id={"rep": partner}, device_id_type=MESH)

    def each(first, last, action):
        def body(i, carry):
            action(i)
            return carry

        lax.fori_loop(first, last, body, 0)

    def each_peer(action):
        step = BURST if (peers - 1) % BURST == 0 else 1

        def burst(i):
            for k in range(step):
                action(1 + i * step + k)

        each(0, (peers - 1) // step, burst)

    def greet(d):
        pl.semaphore_signal(
            barrier, inc=1, device_id={"toa": lax.rem(me + d, peers)}, device_id_type=MESH
        )


    small = [
        pltpu.make_async_copy(source, target, small_sems.at[n])
        for n, (source, target) in enumerate(
            [
                (pulsar_hbm, pulsar_ref),
                (backend_hbm, backend_ref),
                (efac_hbm, efac_ref),
                (equad_hbm, equad_ref),
                (counts_hbm, counts_ref),
                (slot_hbm, slot_ref),
                (error_hbm, error_ref),
                (residual_hbm, residual_ref),
            ]
        )
    ]
    for copy in small:
        copy.start()
    each_peer(greet)

    def chunk(ref, g):
        return ref.at[:, pl.ds(pl.multiple_of(g * group, group), group), :]

    def load(g):
        return pltpu.make_async_copy(chunk(basis_ref, g), chunk(own_store, g), load_sems.at[g])

    def turn(p):
        return lax.rem(partner * swaps + p, steps)

    each(0, steps, lambda p: load(turn(p)).start())

    def swap(g):
        return pltpu.make_async_remote_copy(
            src_ref=chunk(own_store, partner * swaps + g),
            dst_ref=chunk(other_store, g),
            send_sem=sends.at[SWAP],
            recv_sem=swap_arrivals.at[g],
            device_id={"rep": partner},
            device_id_type=MESH,
        )


    for wide in (wide_even, wide_odd):
        for c in range(cuts):
            wide[c, half * PITCH :, :] = jnp.zeros(((span - half) * PITCH, LANES), f32)
    for copy in small[:-2]:
        copy.wait()

    def onehot(row, amount):
        index = lax.broadcasted_iota(jnp.int32, (amount, row.shape[1]), 0)
        return (index == row).astype(f32)

    pulsar_hot = onehot(pulsar_ref[...], pulsar_total)
    backend_hot = onehot(backend_ref[...], efac_ref.shape[1])

    def terms_of(values):
        high = values.astype(bf16)
        rest = values - high.astype(f32)
        middle = rest.astype(bf16)
        return [high, middle, (rest - middle.astype(f32)).astype(bf16)]

    def lookup(ref):
        table = jnp.concatenate(terms_of(ref[...]), axis=0)
        hot = jnp.concatenate([pulsar_hot.astype(bf16)] * 3, axis=0)
        columns = contract(table, hot, ((0,), (0,)))
        return jnp.sum(columns * backend_hot, axis=0, keepdims=True)

    factor = lookup(efac_ref)
    floor_term = lookup(equad_ref)
    stacked = jnp.concatenate(
        [
            factor * factor,
            floor_term * floor_term,
            counts_ref[...].astype(f32),
            jnp.zeros((5, tile_total), f32),
        ],
        axis=0,
    )
    columns = jnp.transpose(stacked)
    slot = slot_ref[...]
    dest = slot // tile_total
    place = (slot - dest * tile_total).astype(f32)
    dest_hot = onehot(dest, peers)
    earlier = (
        lax.broadcasted_iota(jnp.int32, (tile_total, tile_total), 0)
        < lax.broadcasted_iota(jnp.int32, (tile_total, tile_total), 1)
    ).astype(bf16)
    before = contract(dest_hot.astype(bf16), earlier, ((1,), (0,)))
    rank = jnp.sum(before * dest_hot, axis=0, keepdims=True)
    position = lax.rem(dest - me + peers, peers) * per_peer + rank.astype(jnp.int32)
    order = onehot(position, tile_total).astype(bf16)
    places = contract((dest_hot * place).astype(bf16), order, ((1,), (1,)))
    places_ref[...] = jnp.repeat(places, owned, axis=0) if owned > 1 else places

    evens = lax.broadcasted_iota(jnp.int32, (tile_total, tile_total), 0)
    pairs = lax.broadcasted_iota(jnp.int32, (tile_total, tile_total), 1)
    count = tile_total // 2
    halves = jnp.where(pairs < count, 2 * pairs, 2 * (pairs - count) + 1)
    parted = contract(pulsar_hot.astype(bf16), (evens == halves).astype(bf16), ((1,), (0,)))
    parted = parted.astype(bf16)
    own_chosen = jnp.concatenate([parted[:, :count], parted[:, count:]], axis=0)
    cross_chosen = jnp.where(core == 0, own_chosen[:, : count // 2], own_chosen[:, count // 2 :])
    for copy in small[-2:]:
        copy.wait()
    lane = lax.broadcasted_iota(jnp.int32, (tile_total, row_total), 1).astype(f32)
    error = error_ref[...]
    weight = jnp.where(
        lane < columns[:, 2:3], 1.0 / (columns[:, 0:1] * (error * error) + columns[:, 1:2]), 0.0
    )
    weights[...] = weight

    white = jnp.sqrt(weight) * residual_ref[...]
    ordered = contract(order, white.astype(bf16), ((1,), (0,)))
    ordered = ordered.reshape(peers, per_peer, row_total)
    pieces = [ordered[:, :, c * LANES : (c + 1) * LANES] for c in range(cuts)]
    unused = sorted_rows.shape[1] - cuts * per_peer
    if unused:
        pieces.append(jnp.zeros((peers, unused, LANES), f32))
    message = jnp.concatenate(pieces, axis=1).astype(bf16)
    sorted_rows[...] = message
    got_rows[0] = message[0]

    def remote(source, target, n, d):
        return pltpu.make_async_remote_copy(
            src_ref=source,
            dst_ref=target.at[d],
            send_sem=sends.at[n],
            recv_sem=arrivals.at[n],
            device_id={"toa": lax.rem(me + d, peers)},
            device_id_type=MESH,
        )

    def arrived(target, n):
        rest = target.at[pl.ds(1, peers - 1)]
        pltpu.make_async_copy(rest, rest, arrivals.at[n]).wait()

    def gone(target, n):
        rest = target.at[pl.ds(1, peers - 1)]
        pltpu.make_async_copy(rest, rest, sends.at[n]).wait()

    def send_rows(d):
        remote(sorted_rows.at[d], got_rows, ROWS, d).start()


    def spread(ref, g, wide, piece=0, pieces=1):
        start = pl.multiple_of(g * group, group)
        for j in range(half * piece // pieces, half * (piece + 1) // pieces):
            block = ref[j, pl.ds(start, group), :].astype(f32)
            at = j * PITCH
            for c in range(cuts):
                wide[c, at : at + group, :] = block[:, c * LANES : (c + 1) * LANES]

    def columns_of(wide, i):
        return jnp.concatenate(
            [wide[c, pl.ds(i, span, stride=PITCH), :] for c in range(cuts)], axis=1
        )

    starts = half // 8 * 8
    below = lax.broadcasted_iota(jnp.int32, (span - starts, row_total), 0) == half - starts
    first_lanes = lax.broadcasted_iota(jnp.int32, (span, 2 * span), 1) < span
    unused_lanes = jnp.zeros((span, LANES - 2 * span), f32)

    def multiply(grams, g, step, left, right):
        both = contract(left, right, ((1,), (1,)))
        both = jnp.where(first_lanes, both[:span], both[span:])
        row = pl.multiple_of(g * (group // 2 * apart), 8) + step * apart
        grams[pl.ds(row, span), :] = jnp.concatenate([both, unused_lanes], axis=1)

    def own_chunk(p, wide, other, keep):
        g = turn(p)
        later = turn(jnp.minimum(p + 1, steps - 1))
        start = pl.multiple_of(g * group, group)
        weight = weights[pl.ds(start, group), :]
        residual = residual_ref[pl.ds(start, group), :]
        spread(own_store, later, other)
        for i in range(0, group, 2):
            bases = [columns_of(wide, k) for k in (i, i + 1)]
            scaled = []
            for k, basis in zip((i, i + 1), bases):
                with_residual = jnp.where(below, residual[k : k + 1, :], basis[starts:])
                one = jnp.concatenate([basis[:starts], with_residual], axis=0)
                scaled.append(weight[k : k + 1, :] * one)
            left = jnp.concatenate(scaled, axis=0).astype(bf16)
            if keep:
                lefts[(p - swaps) * (group // 2) + i // 2] = left
            right = jnp.concatenate(bases, axis=0).astype(bf16)
            multiply(own_grams, g, i // 2, left, right)

    def cross_chunk(g):
        spread(other_store, g, wide_even)
        for i in range(0, group, 2):
            bases = [columns_of(wide_even, k) for k in (i, i + 1)]
            right = jnp.concatenate(bases, axis=0).astype(bf16)
            multiply(cross_grams, g, i // 2, lefts[g * (group // 2) + i // 2], right)

    lanes = lax.broadcasted_iota(jnp.int32, (pulsar_total, LANES), 1)
    low_lanes = lanes < span
    inner = jnp.where(low_lanes, lanes, lanes - span)

    def picked(grams, chosen, j):
        return grams[pl.ds(j, chosen.shape[1], stride=apart), :]

    def joined(out):
        return out[:pulsar_total], out[pulsar_total:]

    def summed(grams, chosen, slots):
        sides = [picked(grams, chosen, slot).astype(bf16) for slot in slots]
        even, odd = joined(contract(chosen, jnp.concatenate(sides, axis=1), ((1,), (0,))))
        return [
            jnp.where(low_lanes, even[:, at : at + LANES], odd[:, at : at + LANES])
            for at in range(0, len(slots) * LANES, LANES)
        ]

    def fold(low, high):
        low = low + pltpu.roll(low, LANES - span, 1)
        high = high + pltpu.roll(high, span, 1)
        return jnp.where(low_lanes, low, high)

    def put(row, value):
        part_wide[pl.ds(row, pulsar_total, stride=apart_part), :] = value

    def settle(target):
        count = target.shape[1]
        for p in range(pulsar_total):
            target[p] = part_wide[p * apart_part : p * apart_part + count, :].astype(bf16)

    zero = jnp.zeros((pulsar_total, LANES), f32)

    def gather_own():
        diagonal = zero
        merged = []
        for j in range(side):
            if j >= half - side:
                merged.append(summed(own_grams, own_chosen, (j,))[0])
            else:
                first, second = summed(own_grams, own_chosen, (j, side + j))
                diagonal = diagonal + jnp.where(inner == side + j, second, 0.0)
                second = pltpu.roll(second, LANES - side, 1)
                merged.append(jnp.where((inner > j) & (inner < side), second, first))
        for j in range(quarter - 1):
            put(j, fold(merged[j], merged[j + quarter]))
        put(quarter - 1, fold(merged[quarter - 1], diagonal))
        put(quarter, projections())
        for row in range(quarter + 1, SHORT - 1):
            put(row, zero)
        put(SHORT - 1, places_ref[...])
        settle(own_part)

    def gather_cross():
        for r in range(side):
            slots = [j for j in (r, r + side) if j < half]
            found = summed(cross_grams, cross_chosen, slots) + [zero] * (2 - len(slots))
            put(r, fold(found[0], found[1]))
        for r in range(side, TALL):
            put(r, zero)
        settle(cross_part)

    def projections():
        terms = picked(own_grams, own_chosen, half)
        high = terms.astype(bf16)
        low = (terms - high.astype(f32)).astype(bf16)
        doubled = jnp.concatenate([own_chosen, own_chosen], axis=1)
        even, odd = joined(contract(doubled, jnp.concatenate([high, low], axis=0), ((1,), (0,))))
        value = fold(jnp.where(low_lanes, even, odd), zero)
        coarse = value.astype(bf16).astype(f32)
        return jnp.where(low_lanes, coarse, pltpu.roll(value - coarse, span, 1))

    def send_part(part, target, n):
        def one(k):
            e = jnp.where(k <= me, k - 1, k)
            d = jnp.where(k <= me, k - 1 - me + peers, k - me)
            pltpu.make_async_remote_copy(
                src_ref=part.at[pl.ds(e * owned, owned)],
                dst_ref=target.at[d],
                send_sem=sends.at[n],
                recv_sem=arrivals.at[n],
                device_id={"toa": e},
                device_id_type=MESH,
            ).start()

        each_peer(one)

    def total(part, target):
        mine = part[pl.ds(me * owned, owned)].astype(f32)
        return mine + jnp.sum(target[pl.ds(1, peers - 1)].astype(f32), axis=0)

    def own_chunks(keep, h):
        @pl.when(keep)
        def _():
            load(turn(2 * h + 1)).wait()

        @pl.when((h < steps // 2 - 1) & (2 * h + 2 >= swaps))
        def _():
            load(turn(2 * h + 2)).wait()

        own_chunk(2 * h, wide_even, wide_odd, keep)
        own_chunk(2 * h + 1, wide_odd, wide_even, keep)

    load(turn(0)).wait()
    spread(own_store, turn(0), wide_even)
    pl.semaphore_wait(barrier, peers)
    each_peer(send_rows)
    each(1, swaps, lambda p: load(turn(p)).wait())
    each(0, swaps, lambda g: swap(g).start())
    each(0, steps // 4, functools.partial(own_chunks, False))
    each(steps // 4, steps // 2, functools.partial(own_chunks, True))
    swap(0).wait_recv()
    gather_own()
    cross_chunk(0)
    send_part(own_part, got_own, OWN)

    for g in range(1, swaps):
        swap(g).wait_recv()
        cross_chunk(g)
    gather_cross()
    send_part(cross_part, got_cross, CROSS)

    def to_partner(source, target, n):
        return pltpu.make_async_remote_copy(
            src_ref=source,
            dst_ref=target,
            send_sem=sends.at[n],
            recv_sem=arrivals.at[n],
            device_id={"rep": partner},
            device_id_type=MESH,
        )

    arrived(got_cross, CROSS)
    cross_sum[...] = total(cross_part, got_cross)
    last = to_partner(cross_sum, partner_sum, LAST)
    last.start()
    everything = other_store
    pltpu.make_async_copy(everything, everything, sends.at[SWAP]).wait()
    arrived(got_rows, ROWS)
    arrived(got_own, OWN)
    own_sum = total(own_part, got_own)
    home = onehot(own_sum[0][SHORT - 1 : SHORT].astype(jnp.int32), tile_total)
    messages = got_rows[...].astype(f32)
    for c in range(cuts):
        rows = messages[:, c * per_peer : (c + 1) * per_peer, :].reshape(tile_total, LANES)
        white_ref[:, c * LANES : (c + 1) * LANES] = contract(
            home.astype(bf16), rows.astype(bf16), ((1,), (0,))
        )
    row_at = lax.broadcasted_iota(jnp.int32, (TALL, TALL), 0)
    lane_at = lax.broadcasted_iota(jnp.int32, (TALL, TALL), 1)
    place_at = lax.broadcasted_iota(jnp.int32, (span, LANES), 1)
    rest = half - side

    for q in range(owned):
        block = own_sum[q]
        high = pltpu.roll(block, LANES - span, 1)
        rows = [block[:quarter], high[: side - quarter], jnp.zeros((TALL - side, LANES), f32)]
        rows = jnp.concatenate(rows, axis=0)
        merged = rows[:, :TALL]
        mixed = rows[:, side : side + TALL]
        turned = jnp.transpose(merged)
        diagonal = high[quarter - 1 : quarter, side : side + TALL]
        upper = jnp.where(lane_at < row_at, turned, diagonal)
        upper = jnp.where(lane_at > row_at, merged, upper)
        lower = jnp.where(lane_at <= row_at, merged, turned)
        own_square[q, :side, :side] = lower[:side, :side]
        own_square[q, :side, side:half] = mixed[:side, :rest]
        own_square[q, side:half, :side] = jnp.transpose(mixed)[:rest, :side]
        own_square[q, side:half, side:half] = upper[:rest, :rest]
        square = own_square[q]
        own_square[q] = jnp.where(core == 0, square, pltpu.roll(square, half, 1))
        found = block[quarter : quarter + 1] + high[quarter : quarter + 1]
        projection_ref[q : q + 1, :] = found[:, :half]

    def unfold(block):
        tall = [block[:side, :span], block[:rest, span : 2 * span]]
        return jnp.concatenate(tall + [jnp.zeros((span - half, span), f32)], axis=0)

    for target, n in ((got_rows, ROWS), (got_own, OWN), (got_cross, CROSS)):
        gone(target, n)
    last.wait()
    for q in range(owned):
        both = unfold(cross_sum[q]) + jnp.transpose(unfold(partner_sum[q]))
        both = jnp.concatenate([both, jnp.zeros((span, LANES - span), f32)], axis=1)
        both = jnp.where(core == 0, pltpu.roll(both, half, 1), both)
        mine = (place_at < half) == (core == 0)
        gram_ref[:, q, :] = jnp.where(mine, own_square[q], both)[:half, : 2 * half]


def finish_kernel(gram_in, projection_in, white_in, gram_out, projection_out, white_out, sems):
    copies = [
        pltpu.make_async_copy(source, target, sems.at[n])
        for n, (source, target) in enumerate(
            [(white_in, white_out), (gram_in, gram_out), (projection_in, projection_out)]
        )
    ]
    for copy in copies:
        copy.start()
    for copy in copies:
        copy.wait()


def shards(
    residual, toa_error, basis_rows, efac_table, equad_table, pulsar, backend, counts, owner_slot
):
    tile_total, row_total = residual.shape
    peers = lax.axis_size("toa")
    half = basis_rows.shape[1]
    pulsar_total, backend_total = efac_table.shape
    owned = pulsar_total // peers
    per_peer = tile_total // peers
    group = min(GROUP, tile_total)
    steps = tile_total // group
    cuts = row_total // LANES
    span = round_up(half + 1, 8)
    message = round_up(cuts * per_peer, 16)
    f32 = jnp.float32
    bf16 = jnp.bfloat16
    i32 = jnp.int32
    anywhere = pl.BlockSpec(memory_space=pltpu.HBM)
    vmem = pl.BlockSpec(memory_space=pltpu.VMEM)

    def row(vector):
        return vector.reshape(1, tile_total)

    results = [
        ((half, owned, 2 * half), f32),
        ((owned, half), f32),
        ((tile_total, row_total), f32),
    ]
    held = pl.pallas_call(
        functools.partial(whole_kernel, peers),
        in_specs=[anywhere] * 9,
        out_specs=[vmem] * 3,
        out_shape=[pltpu.VMEM(shape, dtype) for shape, dtype in results],
        scratch_shapes=[
            pltpu.VMEM((1, tile_total), i32),
            pltpu.VMEM((1, tile_total), i32),
            pltpu.VMEM((1, tile_total), i32),
            pltpu.VMEM((1, tile_total), i32),
            pltpu.VMEM((pulsar_total, backend_total), f32),
            pltpu.VMEM((pulsar_total, backend_total), f32),
            pltpu.VMEM((tile_total, row_total), f32),
            pltpu.VMEM((tile_total, row_total), f32),
            pltpu.VMEM((peers, message, LANES), bf16),
            pltpu.VMEM((peers, message, LANES), bf16),
            pltpu.VMEM((pulsar_total, tile_total), f32),
            pltpu.VMEM((half, tile_total, row_total), bf16),
            pltpu.VMEM((half, tile_total // 2, row_total), bf16),
            pltpu.VMEM((tile_total, row_total), f32),
            pltpu.VMEM((cuts, span * PITCH, LANES), f32),
            pltpu.VMEM((cuts, span * PITCH, LANES), f32),
            pltpu.VMEM((tile_total // 4, 2 * span, row_total), bf16),
            pltpu.VMEM((tile_total // 2 * (span + 1), LANES), f32),
            pltpu.VMEM((tile_total // 4 * (span + 1), LANES), f32),
            pltpu.VMEM((pulsar_total * (TALL + 1), LANES), f32),
            pltpu.VMEM((pulsar_total, SHORT, LANES), bf16),
            pltpu.VMEM((pulsar_total, TALL, LANES), bf16),
            pltpu.VMEM((peers, owned, SHORT, LANES), bf16),
            pltpu.VMEM((peers, owned, TALL, LANES), bf16),
            pltpu.VMEM((owned, TALL, LANES), f32),
            pltpu.VMEM((owned, TALL, LANES), f32),
            pltpu.VMEM((owned, span, LANES), f32),
            pltpu.SemaphoreType.DMA((8,)),
            pltpu.SemaphoreType.DMA((steps,)),
            pltpu.SemaphoreType.DMA((steps // 2,)),
            pltpu.SemaphoreType.DMA((5,)),
            pltpu.SemaphoreType.DMA((5,)),
        ],
        compiler_params=pltpu.CompilerParams(
            collective_id=0, has_side_effects=True, vmem_limit_bytes=VMEM_KERNEL
        ),
        name="whole",
    )(
        *[
            pltpu.with_memory_space_constraint(value, pltpu.HBM)
            for value in (
                row(pulsar),
                row(backend),
                row(counts),
                row(owner_slot),
                efac_table,
                equad_table,
                residual,
                toa_error,
                jnp.transpose(basis_rows, (1, 0, 2)),
            )
        ]
    )
    gram, projection, whitened = pl.pallas_call(
        finish_kernel,
        in_specs=[vmem] * 3,
        out_specs=[anywhere] * 3,
        out_shape=[jax.ShapeDtypeStruct(shape, dtype) for shape, dtype in results],
        scratch_shapes=[pltpu.SemaphoreType.DMA((3,))],
        name="finish",
    )(*[pltpu.with_memory_space_constraint(value, pltpu.VMEM) for value in held])
    return (jnp.transpose(gram, (1, 2, 0)), projection, whitened)


def solution(mesh):
    in_specs = (
        P("toa", None),
        P("toa", None),
        P("toa", "rep", None),
        P(),
        P(),
        P("toa"),
        P("toa"),
        P("toa"),
        P("toa"),
    )
    out_specs = (P("toa", None, "rep"), P("toa", "rep"), P("toa", None))
    return jax.shard_map(shards, mesh=mesh, in_specs=in_specs, out_specs=out_specs, check_vma=False)
```

```python
import functools

import jax
import jax.numpy as jnp
from jax import lax
from jax.experimental import pallas as pl
from jax.experimental.pallas import tpu as pltpu
from jax.sharding import PartitionSpec as P

MESH = pl.DeviceIdType.MESH
GROUP = 16
BURST = 15
LANES = 128
PITCH = GROUP + 1
SHORT = 16
TALL = 32
VMEM_KERNEL = 48 * 1024 * 1024
SWAP, ROWS, OWN, CROSS, LAST = range(5)


def round_up(value, step):
    return (value + step - 1) // step * step


def contract(left, right, dims):
    return lax.dot_general(
        left, right, (dims, ((), ())), preferred_element_type=jnp.float32
    )


def whole_kernel(
    peers,
    pulsar_hbm,
    backend_hbm,
    counts_hbm,
    slot_hbm,
    efac_hbm,
    equad_hbm,
    residual_hbm,
    error_hbm,
    basis_ref,
    gram_ref,
    projection_ref,
    white_ref,
    pulsar_ref,
    backend_ref,
    counts_ref,
    slot_ref,
    efac_ref,
    equad_ref,
    residual_ref,
    error_ref,
    sorted_rows,
    got_rows,
    places_ref,
    own_store,
    other_store,
    weights,
    wide_even,
    wide_odd,
    lefts,
    own_grams,
    cross_grams,
    part_wide,
    own_part,
    cross_part,
    got_own,
    got_cross,
    cross_sum,
    partner_sum,
    own_square,
    small_sems,
    load_sems,
    swap_arrivals,
    sends,
    arrivals,
):
    me = lax.axis_index("toa")
    core = lax.axis_index("rep")
    partner = 1 - core
    half, tile_total, row_total = basis_ref.shape
    pulsar_total = efac_hbm.shape[0]
    owned = pulsar_total // peers
    per_peer = tile_total // peers
    group = min(GROUP, tile_total)
    steps = tile_total // group
    swaps = steps // 2
    cuts = row_total // LANES
    side = (half + 1) // 2
    quarter = (side + 1) // 2
    span = round_up(half + 1, 8)
    apart = span + 1
    apart_part = TALL + 1
    f32 = jnp.float32
    bf16 = jnp.bfloat16

    barrier = pltpu.get_barrier_semaphore()
    pl.semaphore_signal(barrier, inc=1, device_id={"rep": partner}, device_id_type=MESH)

    def each(first, last, action):
        def body(i, carry):
            action(i)
            return carry

        lax.fori_loop(first, last, body, 0)

    def each_peer(action):
        step = BURST if (peers - 1) % BURST == 0 else 1

        def burst(i):
            for k in range(step):
                action(1 + i * step + k)

        each(0, (peers - 1) // step, burst)

    def greet(d):
        pl.semaphore_signal(
            barrier, inc=1, device_id={"toa": lax.rem(me + d, peers)}, device_id_type=MESH
        )


    small = [
        pltpu.make_async_copy(source, target, small_sems.at[n])
        for n, (source, target) in enumerate(
            [
                (pulsar_hbm, pulsar_ref),
                (backend_hbm, backend_ref),
                (efac_hbm, efac_ref),
                (equad_hbm, equad_ref),
                (counts_hbm, counts_ref),
                (slot_hbm, slot_ref),
                (error_hbm, error_ref),
                (residual_hbm, residual_ref),
            ]
        )
    ]
    for copy in small:
        copy.start()
    each_peer(greet)

    def chunk(ref, g):
        return ref.at[:, pl.ds(pl.multiple_of(g * group, group), group), :]

    def load(g):
        return pltpu.make_async_copy(chunk(basis_ref, g), chunk(own_store, g), load_sems.at[g])

    def turn(p):
        return lax.rem(partner * swaps + p, steps)

    each(0, steps, lambda p: load(turn(p)).start())

    def swap(g):
        return pltpu.make_async_remote_copy(
            src_ref=chunk(own_store, partner * swaps + g),
            dst_ref=chunk(other_store, g),
            send_sem=sends.at[SWAP],
            recv_sem=swap_arrivals.at[g],
            device_id={"rep": partner},
            device_id_type=MESH,
        )


    for wide in (wide_even, wide_odd):
        for c in range(cuts):
            wide[c, half * PITCH :, :] = jnp.zeros(((span - half) * PITCH, LANES), f32)
    for copy in small[:-2]:
        copy.wait()

    def onehot(row, amount):
        index = lax.broadcasted_iota(jnp.int32, (amount, row.shape[1]), 0)
        return (index == row).astype(f32)

    pulsar_hot = onehot(pulsar_ref[...], pulsar_total)
    backend_hot = onehot(backend_ref[...], efac_ref.shape[1])

    def terms_of(values):
        high = values.astype(bf16)
        rest = values - high.astype(f32)
        middle = rest.astype(bf16)
        return [high, middle, (rest - middle.astype(f32)).astype(bf16)]

    def lookup(ref):
        table = jnp.concatenate(terms_of(ref[...]), axis=0)
        hot = jnp.concatenate([pulsar_hot.astype(bf16)] * 3, axis=0)
        columns = contract(table, hot, ((0,), (0,)))
        return jnp.sum(columns * backend_hot, axis=0, keepdims=True)

    factor = lookup(efac_ref)
    floor_term = lookup(equad_ref)
    stacked = jnp.concatenate(
        [
            factor * factor,
            floor_term * floor_term,
            counts_ref[...].astype(f32),
            jnp.zeros((5, tile_total), f32),
        ],
        axis=0,
    )
    columns = jnp.transpose(stacked)
    slot = slot_ref[...]
    dest = slot // tile_total
    place = (slot - dest * tile_total).astype(f32)
    dest_hot = onehot(dest, peers)
    earlier = (
        lax.broadcasted_iota(jnp.int32, (tile_total, tile_total), 0)
        < lax.broadcasted_iota(jnp.int32, (tile_total, tile_total), 1)
    ).astype(bf16)
    before = contract(dest_hot.astype(bf16), earlier, ((1,), (0,)))
    rank = jnp.sum(before * dest_hot, axis=0, keepdims=True)
    position = lax.rem(dest - me + peers, peers) * per_peer + rank.astype(jnp.int32)
    order = onehot(position, tile_total).astype(bf16)
    places = contract((dest_hot * place).astype(bf16), order, ((1,), (1,)))
    places_ref[...] = jnp.repeat(places, owned, axis=0) if owned > 1 else places

    evens = lax.broadcasted_iota(jnp.int32, (tile_total, tile_total), 0)
    pairs = lax.broadcasted_iota(jnp.int32, (tile_total, tile_total), 1)
    count = tile_total // 2
    halves = jnp.where(pairs < count, 2 * pairs, 2 * (pairs - count) + 1)
    parted = contract(pulsar_hot.astype(bf16), (evens == halves).astype(bf16), ((1,), (0,)))
    parted = parted.astype(bf16)
    own_chosen = jnp.concatenate([parted[:, :count], parted[:, count:]], axis=0)
    cross_chosen = jnp.where(core == 0, own_chosen[:, : count // 2], own_chosen[:, count // 2 :])
    for copy in small[-2:]:
        copy.wait()
    lane = lax.broadcasted_iota(jnp.int32, (tile_total, row_total), 1).astype(f32)
    error = error_ref[...]
    weight = jnp.where(
        lane < columns[:, 2:3], 1.0 / (columns[:, 0:1] * (error * error) + columns[:, 1:2]), 0.0
    )
    weights[...] = weight

    white = jnp.sqrt(weight) * residual_ref[...]
    ordered = contract(order, white.astype(bf16), ((1,), (0,)))
    ordered = ordered.reshape(peers, per_peer, row_total)
    pieces = [ordered[:, :, c * LANES : (c + 1) * LANES] for c in range(cuts)]
    unused = sorted_rows.shape[1] - cuts * per_peer
    if unused:
        pieces.append(jnp.zeros((peers, unused, LANES), f32))
    message = jnp.concatenate(pieces, axis=1).astype(bf16)
    sorted_rows[...] = message
    got_rows[0] = message[0]

    def remote(source, target, n, d):
        return pltpu.make_async_remote_copy(
            src_ref=source,
            dst_ref=target.at[d],
            send_sem=sends.at[n],
            recv_sem=arrivals.at[n],
            device_id={"toa": lax.rem(me + d, peers)},
            device_id_type=MESH,
        )

    def arrived(target, n):
        rest = target.at[pl.ds(1, peers - 1)]
        pltpu.make_async_copy(rest, rest, arrivals.at[n]).wait()

    def gone(target, n):
        rest = target.at[pl.ds(1, peers - 1)]
        pltpu.make_async_copy(rest, rest, sends.at[n]).wait()

    def send_rows(d):
        remote(sorted_rows.at[d], got_rows, ROWS, d).start()


    def spread(ref, g, wide, piece=0, pieces=1):
        start = pl.multiple_of(g * group, group)
        for j in range(half * piece // pieces, half * (piece + 1) // pieces):
            block = ref[j, pl.ds(start, group), :].astype(f32)
            at = j * PITCH
            for c in range(cuts):
                wide[c, at : at + group, :] = block[:, c * LANES : (c + 1) * LANES]

    def columns_of(wide, i):
        return jnp.concatenate(
            [wide[c, pl.ds(i, span, stride=PITCH), :] for c in range(cuts)], axis=1
        )

    starts = half // 8 * 8
    below = lax.broadcasted_iota(jnp.int32, (span - starts, row_total), 0) == half - starts
    first_lanes = lax.broadcasted_iota(jnp.int32, (span, 2 * span), 1) < span
    unused_lanes = jnp.zeros((span, LANES - 2 * span), f32)

    def multiply(grams, g, step, left, right):
        both = contract(left, right, ((1,), (1,)))
        both = jnp.where(first_lanes, both[:span], both[span:])
        row = pl.multiple_of(g * (group // 2 * apart), 8) + step * apart
        grams[pl.ds(row, span), :] = jnp.concatenate([both, unused_lanes], axis=1)

    def own_chunk(p, wide, other, keep):
        g = turn(p)
        later = turn(jnp.minimum(p + 1, steps - 1))
        start = pl.multiple_of(g * group, group)
        weight = weights[pl.ds(start, group), :]
        residual = residual_ref[pl.ds(start, group), :]
        spread(own_store, later, other)
        for i in range(0, group, 2):
            bases = [columns_of(wide, k) for k in (i, i + 1)]
            scaled = []
            for k, basis in zip((i, i + 1), bases):
                with_residual = jnp.where(below, residual[k : k + 1, :], basis[starts:])
                one = jnp.concatenate([basis[:starts], with_residual], axis=0)
                scaled.append(weight[k : k + 1, :] * one)
            left = jnp.concatenate(scaled, axis=0).astype(bf16)
            if keep:
                lefts[(p - swaps) * (group // 2) + i // 2] = left
            right = jnp.concatenate(bases, axis=0).astype(bf16)
            multiply(own_grams, g, i // 2, left, right)

    def cross_chunk(g):
        spread(other_store, g, wide_even)
        for i in range(0, group, 2):
            bases = [columns_of(wide_even, k) for k in (i, i + 1)]
            right = jnp.concatenate(bases, axis=0).astype(bf16)
            multiply(cross_grams, g, i // 2, lefts[g * (group // 2) + i // 2], right)

    lanes = lax.broadcasted_iota(jnp.int32, (pulsar_total, LANES), 1)
    low_lanes = lanes < span
    inner = jnp.where(low_lanes, lanes, lanes - span)

    def picked(grams, chosen, j):
        return grams[pl.ds(j, chosen.shape[1], stride=apart), :]

    def joined(out):
        return out[:pulsar_total], out[pulsar_total:]

    def summed(grams, chosen, slots):
        sides = [picked(grams, chosen, slot).astype(bf16) for slot in slots]
        even, odd = joined(contract(chosen, jnp.concatenate(sides, axis=1), ((1,), (0,))))
        return [
            jnp.where(low_lanes, even[:, at : at + LANES], odd[:, at : at + LANES])
            for at in range(0, len(slots) * LANES, LANES)
        ]

    def fold(low, high):
        low = low + pltpu.roll(low, LANES - span, 1)
        high = high + pltpu.roll(high, span, 1)
        return jnp.where(low_lanes, low, high)

    def put(row, value):
        part_wide[pl.ds(row, pulsar_total, stride=apart_part), :] = value

    def settle(target):
        count = target.shape[1]
        for p in range(pulsar_total):
            target[p] = part_wide[p * apart_part : p * apart_part + count, :].astype(bf16)

    zero = jnp.zeros((pulsar_total, LANES), f32)

    def gather_own():
        diagonal = zero
        merged = []
        for j in range(side):
            if j >= half - side:
                merged.append(summed(own_grams, own_chosen, (j,))[0])
            else:
                first, second = summed(own_grams, own_chosen, (j, side + j))
                diagonal = diagonal + jnp.where(inner == side + j, second, 0.0)
                second = pltpu.roll(second, LANES - side, 1)
                merged.append(jnp.where((inner > j) & (inner < side), second, first))
        for j in range(quarter - 1):
            put(j, fold(merged[j], merged[j + quarter]))
        put(quarter - 1, fold(merged[quarter - 1], diagonal))
        put(quarter, projections())
        for row in range(quarter + 1, SHORT - 1):
            put(row, zero)
        put(SHORT - 1, places_ref[...])
        settle(own_part)

    def gather_cross():
        for r in range(side):
            slots = [j for j in (r, r + side) if j < half]
            found = summed(cross_grams, cross_chosen, slots) + [zero] * (2 - len(slots))
            put(r, fold(found[0], found[1]))
        for r in range(side, TALL):
            put(r, zero)
        settle(cross_part)

    def projections():
        terms = picked(own_grams, own_chosen, half)
        high = terms.astype(bf16)
        low = (terms - high.astype(f32)).astype(bf16)
        doubled = jnp.concatenate([own_chosen, own_chosen], axis=1)
        even, odd = joined(contract(doubled, jnp.concatenate([high, low], axis=0), ((1,), (0,))))
        value = fold(jnp.where(low_lanes, even, odd), zero)
        coarse = value.astype(bf16).astype(f32)
        return jnp.where(low_lanes, coarse, pltpu.roll(value - coarse, span, 1))

    def send_part(part, target, n):
        def one(k):
            e = jnp.where(k <= me, k - 1, k)
            d = jnp.where(k <= me, k - 1 - me + peers, k - me)
            pltpu.make_async_remote_copy(
                src_ref=part.at[pl.ds(e * owned, owned)],
                dst_ref=target.at[d],
                send_sem=sends.at[n],
                recv_sem=arrivals.at[n],
                device_id={"toa": e},
                device_id_type=MESH,
            ).start()

        each_peer(one)

    def total(part, target):
        mine = part[pl.ds(me * owned, owned)].astype(f32)
        return mine + jnp.sum(target[pl.ds(1, peers - 1)].astype(f32), axis=0)

    def own_chunks(keep, h):
        @pl.when(keep)
        def _():
            load(turn(2 * h + 1)).wait()

        @pl.when((h < steps // 2 - 1) & (2 * h + 2 >= swaps))
        def _():
            load(turn(2 * h + 2)).wait()

        own_chunk(2 * h, wide_even, wide_odd, keep)
        own_chunk(2 * h + 1, wide_odd, wide_even, keep)

    pl.semaphore_wait(barrier, peers)
    each_peer(send_rows)

    def pass_on(g):
        load(turn(g)).wait()
        swap(g).start()

    each(0, swaps, pass_on)
    spread(own_store, turn(0), wide_even)
    each(0, steps // 4, functools.partial(own_chunks, False))
    each(steps // 4, steps // 2, functools.partial(own_chunks, True))
    swap(0).wait_recv()
    swap(1).wait_recv()
    gather_own()
    cross_chunk(0)
    send_part(own_part, got_own, OWN)
    cross_chunk(1)

    for g in range(2, swaps):
        swap(g).wait_recv()
        cross_chunk(g)
    gather_cross()
    send_part(cross_part, got_cross, CROSS)

    def to_partner(source, target, n):
        return pltpu.make_async_remote_copy(
            src_ref=source,
            dst_ref=target,
            send_sem=sends.at[n],
            recv_sem=arrivals.at[n],
            device_id={"rep": partner},
            device_id_type=MESH,
        )

    arrived(got_cross, CROSS)
    cross_sum[...] = total(cross_part, got_cross)
    last = to_partner(cross_sum, partner_sum, LAST)
    last.start()
    everything = other_store
    pltpu.make_async_copy(everything, everything, sends.at[SWAP]).wait()
    arrived(got_rows, ROWS)
    arrived(got_own, OWN)
    own_sum = total(own_part, got_own)
    home = onehot(own_sum[0][SHORT - 1 : SHORT].astype(jnp.int32), tile_total)
    messages = got_rows[...].astype(f32)
    for c in range(cuts):
        rows = messages[:, c * per_peer : (c + 1) * per_peer, :].reshape(tile_total, LANES)
        white_ref[:, c * LANES : (c + 1) * LANES] = contract(
            home.astype(bf16), rows.astype(bf16), ((1,), (0,))
        )
    row_at = lax.broadcasted_iota(jnp.int32, (TALL, TALL), 0)
    lane_at = lax.broadcasted_iota(jnp.int32, (TALL, TALL), 1)
    place_at = lax.broadcasted_iota(jnp.int32, (span, LANES), 1)
    rest = half - side

    for q in range(owned):
        block = own_sum[q]
        high = pltpu.roll(block, LANES - span, 1)
        rows = [block[:quarter], high[: side - quarter], jnp.zeros((TALL - side, LANES), f32)]
        rows = jnp.concatenate(rows, axis=0)
        merged = rows[:, :TALL]
        mixed = rows[:, side : side + TALL]
        turned = jnp.transpose(merged)
        diagonal = high[quarter - 1 : quarter, side : side + TALL]
        upper = jnp.where(lane_at < row_at, turned, diagonal)
        upper = jnp.where(lane_at > row_at, merged, upper)
        lower = jnp.where(lane_at <= row_at, merged, turned)
        own_square[q, :side, :side] = lower[:side, :side]
        own_square[q, :side, side:half] = mixed[:side, :rest]
        own_square[q, side:half, :side] = jnp.transpose(mixed)[:rest, :side]
        own_square[q, side:half, side:half] = upper[:rest, :rest]
        square = own_square[q]
        own_square[q] = jnp.where(core == 0, square, pltpu.roll(square, half, 1))
        found = block[quarter : quarter + 1] + high[quarter : quarter + 1]
        projection_ref[q : q + 1, :] = found[:, :half]

    def unfold(block):
        tall = [block[:side, :span], block[:rest, span : 2 * span]]
        return jnp.concatenate(tall + [jnp.zeros((span - half, span), f32)], axis=0)

    for target, n in ((got_rows, ROWS), (got_own, OWN), (got_cross, CROSS)):
        gone(target, n)
    last.wait()
    for q in range(owned):
        both = unfold(cross_sum[q]) + jnp.transpose(unfold(partner_sum[q]))
        both = jnp.concatenate([both, jnp.zeros((span, LANES - span), f32)], axis=1)
        both = jnp.where(core == 0, pltpu.roll(both, half, 1), both)
        mine = (place_at < half) == (core == 0)
        gram_ref[:, q, :] = jnp.where(mine, own_square[q], both)[:half, : 2 * half]


def finish_kernel(gram_in, projection_in, white_in, gram_out, projection_out, white_out, sems):
    copies = [
        pltpu.make_async_copy(source, target, sems.at[n])
        for n, (source, target) in enumerate(
            [(white_in, white_out), (gram_in, gram_out), (projection_in, projection_out)]
        )
    ]
    for copy in copies:
        copy.start()
    for copy in copies:
        copy.wait()


def shards(
    residual, toa_error, basis_rows, efac_table, equad_table, pulsar, backend, counts, owner_slot
):
    tile_total, row_total = residual.shape
    peers = lax.axis_size("toa")
    half = basis_rows.shape[1]
    pulsar_total, backend_total = efac_table.shape
    owned = pulsar_total // peers
    per_peer = tile_total // peers
    group = min(GROUP, tile_total)
    steps = tile_total // group
    cuts = row_total // LANES
    span = round_up(half + 1, 8)
    message = round_up(cuts * per_peer, 16)
    f32 = jnp.float32
    bf16 = jnp.bfloat16
    i32 = jnp.int32
    anywhere = pl.BlockSpec(memory_space=pltpu.HBM)
    vmem = pl.BlockSpec(memory_space=pltpu.VMEM)

    def row(vector):
        return vector.reshape(1, tile_total)

    results = [
        ((half, owned, 2 * half), f32),
        ((owned, half), f32),
        ((tile_total, row_total), f32),
    ]
    held = pl.pallas_call(
        functools.partial(whole_kernel, peers),
        in_specs=[anywhere] * 9,
        out_specs=[vmem] * 3,
        out_shape=[pltpu.VMEM(shape, dtype) for shape, dtype in results],
        scratch_shapes=[
            pltpu.VMEM((1, tile_total), i32),
            pltpu.VMEM((1, tile_total), i32),
            pltpu.VMEM((1, tile_total), i32),
            pltpu.VMEM((1, tile_total), i32),
            pltpu.VMEM((pulsar_total, backend_total), f32),
            pltpu.VMEM((pulsar_total, backend_total), f32),
            pltpu.VMEM((tile_total, row_total), f32),
            pltpu.VMEM((tile_total, row_total), f32),
            pltpu.VMEM((peers, message, LANES), bf16),
            pltpu.VMEM((peers, message, LANES), bf16),
            pltpu.VMEM((pulsar_total, tile_total), f32),
            pltpu.VMEM((half, tile_total, row_total), bf16),
            pltpu.VMEM((half, tile_total // 2, row_total), bf16),
            pltpu.VMEM((tile_total, row_total), f32),
            pltpu.VMEM((cuts, span * PITCH, LANES), f32),
            pltpu.VMEM((cuts, span * PITCH, LANES), f32),
            pltpu.VMEM((tile_total // 4, 2 * span, row_total), bf16),
            pltpu.VMEM((tile_total // 2 * (span + 1), LANES), f32),
            pltpu.VMEM((tile_total // 4 * (span + 1), LANES), f32),
            pltpu.VMEM((pulsar_total * (TALL + 1), LANES), f32),
            pltpu.VMEM((pulsar_total, SHORT, LANES), bf16),
            pltpu.VMEM((pulsar_total, TALL, LANES), bf16),
            pltpu.VMEM((peers, owned, SHORT, LANES), bf16),
            pltpu.VMEM((peers, owned, TALL, LANES), bf16),
            pltpu.VMEM((owned, TALL, LANES), f32),
            pltpu.VMEM((owned, TALL, LANES), f32),
            pltpu.VMEM((owned, span, LANES), f32),
            pltpu.SemaphoreType.DMA((8,)),
            pltpu.SemaphoreType.DMA((steps,)),
            pltpu.SemaphoreType.DMA((steps // 2,)),
            pltpu.SemaphoreType.DMA((5,)),
            pltpu.SemaphoreType.DMA((5,)),
        ],
        compiler_params=pltpu.CompilerParams(
            collective_id=0, has_side_effects=True, vmem_limit_bytes=VMEM_KERNEL
        ),
        name="whole",
    )(
        *[
            pltpu.with_memory_space_constraint(value, pltpu.HBM)
            for value in (
                row(pulsar),
                row(backend),
                row(counts),
                row(owner_slot),
                efac_table,
                equad_table,
                residual,
                toa_error,
                jnp.transpose(basis_rows, (1, 0, 2)),
            )
        ]
    )
    gram, projection, whitened = pl.pallas_call(
        finish_kernel,
        in_specs=[vmem] * 3,
        out_specs=[anywhere] * 3,
        out_shape=[jax.ShapeDtypeStruct(shape, dtype) for shape, dtype in results],
        scratch_shapes=[pltpu.SemaphoreType.DMA((3,))],
        name="finish",
    )(*[pltpu.with_memory_space_constraint(value, pltpu.VMEM) for value in held])
    return (jnp.transpose(gram, (1, 2, 0)), projection, whitened)


def solution(mesh):
    in_specs = (
        P("toa", None),
        P("toa", None),
        P("toa", "rep", None),
        P(),
        P(),
        P("toa"),
        P("toa"),
        P("toa"),
        P("toa"),
    )
    out_specs = (P("toa", None, "rep"), P("toa", "rep"), P("toa", None))
    return jax.shard_map(shards, mesh=mesh, in_specs=in_specs, out_specs=out_specs, check_vma=False)
```

```python
import functools

import jax
import jax.numpy as jnp
from jax import lax
from jax.experimental import pallas as pl
from jax.experimental.pallas import tpu as pltpu
from jax.sharding import PartitionSpec as P

MESH = pl.DeviceIdType.MESH
GROUP = 16
BURST = 15
LANES = 128
PITCH = GROUP + 1
SHORT = 16
TALL = 32
VMEM_KERNEL = 48 * 1024 * 1024
SWAP, ROWS, OWN, CROSS, LAST = range(5)


def round_up(value, step):
    return (value + step - 1) // step * step


def contract(left, right, dims):
    return lax.dot_general(
        left, right, (dims, ((), ())), preferred_element_type=jnp.float32
    )


def whole_kernel(
    peers,
    pulsar_hbm,
    backend_hbm,
    counts_hbm,
    slot_hbm,
    efac_hbm,
    equad_hbm,
    residual_hbm,
    error_hbm,
    basis_ref,
    gram_ref,
    projection_ref,
    white_ref,
    pulsar_ref,
    backend_ref,
    counts_ref,
    slot_ref,
    efac_ref,
    equad_ref,
    residual_ref,
    error_ref,
    sorted_rows,
    got_rows,
    places_ref,
    own_store,
    other_store,
    weights,
    wide_even,
    wide_odd,
    lefts,
    own_grams,
    cross_grams,
    part_wide,
    own_part,
    cross_part,
    got_own,
    got_cross,
    cross_sum,
    partner_sum,
    own_square,
    small_sems,
    load_sems,
    swap_arrivals,
    sends,
    arrivals,
):
    me = lax.axis_index("toa")
    core = lax.axis_index("rep")
    partner = 1 - core
    half, tile_total, row_total = basis_ref.shape
    pulsar_total = efac_hbm.shape[0]
    owned = pulsar_total // peers
    per_peer = tile_total // peers
    group = min(GROUP, tile_total)
    steps = tile_total // group
    swaps = steps // 2
    cuts = row_total // LANES
    side = (half + 1) // 2
    quarter = (side + 1) // 2
    span = round_up(half + 1, 8)
    apart = span + 1
    apart_part = TALL + 1
    f32 = jnp.float32
    bf16 = jnp.bfloat16

    barrier = pltpu.get_barrier_semaphore()
    pl.semaphore_signal(barrier, inc=1, device_id={"rep": partner}, device_id_type=MESH)

    def each(first, last, action):
        def body(i, carry):
            action(i)
            return carry

        lax.fori_loop(first, last, body, 0)

    def each_peer(action):
        step = BURST if (peers - 1) % BURST == 0 else 1

        def burst(i):
            for k in range(step):
                action(1 + i * step + k)

        each(0, (peers - 1) // step, burst)

    def greet(d):
        pl.semaphore_signal(
            barrier, inc=1, device_id={"toa": lax.rem(me + d, peers)}, device_id_type=MESH
        )


    small = [
        pltpu.make_async_copy(source, target, small_sems.at[n])
        for n, (source, target) in enumerate(
            [
                (pulsar_hbm, pulsar_ref),
                (backend_hbm, backend_ref),
                (efac_hbm, efac_ref),
                (equad_hbm, equad_ref),
                (counts_hbm, counts_ref),
                (slot_hbm, slot_ref),
                (error_hbm, error_ref),
                (residual_hbm, residual_ref),
            ]
        )
    ]
    for copy in small:
        copy.start()
    each_peer(greet)

    def chunk(ref, g):
        return ref.at[:, pl.ds(pl.multiple_of(g * group, group), group), :]

    def load(g):
        return pltpu.make_async_copy(chunk(basis_ref, g), chunk(own_store, g), load_sems.at[g])

    def turn(p):
        return lax.rem(partner * swaps + p, steps)

    each(0, steps, lambda p: load(turn(p)).start())

    def swap(g):
        return pltpu.make_async_remote_copy(
            src_ref=chunk(own_store, partner * swaps + g),
            dst_ref=chunk(other_store, g),
            send_sem=sends.at[SWAP],
            recv_sem=swap_arrivals.at[g],
            device_id={"rep": partner},
            device_id_type=MESH,
        )


    for wide in (wide_even, wide_odd):
        for c in range(cuts):
            wide[c, half * PITCH :, :] = jnp.zeros(((span - half) * PITCH, LANES), f32)
    for copy in small[:-2]:
        copy.wait()

    def onehot(row, amount):
        index = lax.broadcasted_iota(jnp.int32, (amount, row.shape[1]), 0)
        return (index == row).astype(f32)

    pulsar_hot = onehot(pulsar_ref[...], pulsar_total)
    backend_hot = onehot(backend_ref[...], efac_ref.shape[1])

    def terms_of(values):
        high = values.astype(bf16)
        rest = values - high.astype(f32)
        middle = rest.astype(bf16)
        return [high, middle, (rest - middle.astype(f32)).astype(bf16)]

    def lookup(ref):
        table = jnp.concatenate(terms_of(ref[...]), axis=0)
        hot = jnp.concatenate([pulsar_hot.astype(bf16)] * 3, axis=0)
        columns = contract(table, hot, ((0,), (0,)))
        return jnp.sum(columns * backend_hot, axis=0, keepdims=True)

    factor = lookup(efac_ref)
    floor_term = lookup(equad_ref)
    stacked = jnp.concatenate(
        [
            factor * factor,
            floor_term * floor_term,
            counts_ref[...].astype(f32),
            jnp.zeros((5, tile_total), f32),
        ],
        axis=0,
    )
    columns = jnp.transpose(stacked)
    slot = slot_ref[...]
    dest = slot // tile_total
    place = (slot - dest * tile_total).astype(f32)
    dest_hot = onehot(dest, peers)
    earlier = (
        lax.broadcasted_iota(jnp.int32, (tile_total, tile_total), 0)
        < lax.broadcasted_iota(jnp.int32, (tile_total, tile_total), 1)
    ).astype(bf16)
    before = contract(dest_hot.astype(bf16), earlier, ((1,), (0,)))
    rank = jnp.sum(before * dest_hot, axis=0, keepdims=True)
    position = lax.rem(dest - me + peers, peers) * per_peer + rank.astype(jnp.int32)
    order = onehot(position, tile_total).astype(bf16)
    places = contract((dest_hot * place).astype(bf16), order, ((1,), (1,)))
    places_ref[...] = jnp.repeat(places, owned, axis=0) if owned > 1 else places

    evens = lax.broadcasted_iota(jnp.int32, (tile_total, tile_total), 0)
    pairs = lax.broadcasted_iota(jnp.int32, (tile_total, tile_total), 1)
    count = tile_total // 2
    halves = jnp.where(pairs < count, 2 * pairs, 2 * (pairs - count) + 1)
    parted = contract(pulsar_hot.astype(bf16), (evens == halves).astype(bf16), ((1,), (0,)))
    parted = parted.astype(bf16)
    own_chosen = jnp.concatenate([parted[:, :count], parted[:, count:]], axis=0)
    cross_chosen = jnp.where(core == 0, own_chosen[:, : count // 2], own_chosen[:, count // 2 :])
    for copy in small[-2:]:
        copy.wait()
    lane = lax.broadcasted_iota(jnp.int32, (tile_total, row_total), 1).astype(f32)
    error = error_ref[...]
    weight = jnp.where(
        lane < columns[:, 2:3], 1.0 / (columns[:, 0:1] * (error * error) + columns[:, 1:2]), 0.0
    )
    weights[...] = weight

    white = jnp.sqrt(weight) * residual_ref[...]
    ordered = contract(order, white.astype(bf16), ((1,), (0,)))
    ordered = ordered.reshape(peers, per_peer, row_total)
    pieces = [ordered[:, :, c * LANES : (c + 1) * LANES] for c in range(cuts)]
    unused = sorted_rows.shape[1] - cuts * per_peer
    if unused:
        pieces.append(jnp.zeros((peers, unused, LANES), f32))
    message = jnp.concatenate(pieces, axis=1).astype(bf16)
    sorted_rows[...] = message
    got_rows[0] = message[0]

    def remote(source, target, n, d):
        return pltpu.make_async_remote_copy(
            src_ref=source,
            dst_ref=target.at[d],
            send_sem=sends.at[n],
            recv_sem=arrivals.at[n],
            device_id={"toa": lax.rem(me + d, peers)},
            device_id_type=MESH,
        )

    def arrived(target, n):
        rest = target.at[pl.ds(1, peers - 1)]
        pltpu.make_async_copy(rest, rest, arrivals.at[n]).wait()

    def gone(target, n):
        rest = target.at[pl.ds(1, peers - 1)]
        pltpu.make_async_copy(rest, rest, sends.at[n]).wait()

    def send_rows(d):
        remote(sorted_rows.at[d], got_rows, ROWS, d).start()


    def spread(ref, g, wide, piece=0, pieces=1):
        start = pl.multiple_of(g * group, group)
        for j in range(half * piece // pieces, half * (piece + 1) // pieces):
            block = ref[j, pl.ds(start, group), :].astype(f32)
            at = j * PITCH
            for c in range(cuts):
                wide[c, at : at + group, :] = block[:, c * LANES : (c + 1) * LANES]

    def columns_of(wide, i):
        return jnp.concatenate(
            [wide[c, pl.ds(i, span, stride=PITCH), :] for c in range(cuts)], axis=1
        )

    starts = half // 8 * 8
    below = lax.broadcasted_iota(jnp.int32, (span - starts, row_total), 0) == half - starts
    first_lanes = lax.broadcasted_iota(jnp.int32, (span, 2 * span), 1) < span
    unused_lanes = jnp.zeros((span, LANES - 2 * span), f32)

    def multiply(grams, g, step, left, right):
        both = contract(left, right, ((1,), (1,)))
        both = jnp.where(first_lanes, both[:span], both[span:])
        row = pl.multiple_of(g * (group // 2 * apart), 8) + step * apart
        grams[pl.ds(row, span), :] = jnp.concatenate([both, unused_lanes], axis=1)

    def own_chunk(p, wide, other, keep):
        g = turn(p)
        later = turn(jnp.minimum(p + 1, steps - 1))
        start = pl.multiple_of(g * group, group)
        weight = weights[pl.ds(start, group), :]
        residual = residual_ref[pl.ds(start, group), :]
        spread(own_store, later, other)
        for i in range(0, group, 2):
            bases = [columns_of(wide, k) for k in (i, i + 1)]
            scaled = []
            for k, basis in zip((i, i + 1), bases):
                with_residual = jnp.where(below, residual[k : k + 1, :], basis[starts:])
                one = jnp.concatenate([basis[:starts], with_residual], axis=0)
                scaled.append(weight[k : k + 1, :] * one)
            left = jnp.concatenate(scaled, axis=0).astype(bf16)
            if keep:
                lefts[(p - swaps) * (group // 2) + i // 2] = left
            right = jnp.concatenate(bases, axis=0).astype(bf16)
            multiply(own_grams, g, i // 2, left, right)

    def cross_chunk(g):
        spread(other_store, g, wide_even)
        for i in range(0, group, 2):
            bases = [columns_of(wide_even, k) for k in (i, i + 1)]
            right = jnp.concatenate(bases, axis=0).astype(bf16)
            multiply(cross_grams, g, i // 2, lefts[g * (group // 2) + i // 2], right)

    lanes = lax.broadcasted_iota(jnp.int32, (pulsar_total, LANES), 1)
    low_lanes = lanes < span
    inner = jnp.where(low_lanes, lanes, lanes - span)

    def picked(grams, chosen, j):
        return grams[pl.ds(j, chosen.shape[1], stride=apart), :]

    def joined(out):
        return out[:pulsar_total], out[pulsar_total:]

    def summed(grams, chosen, slots):
        sides = [picked(grams, chosen, slot).astype(bf16) for slot in slots]
        even, odd = joined(contract(chosen, jnp.concatenate(sides, axis=1), ((1,), (0,))))
        return [
            jnp.where(low_lanes, even[:, at : at + LANES], odd[:, at : at + LANES])
            for at in range(0, len(slots) * LANES, LANES)
        ]

    def fold(low, high):
        low = low + pltpu.roll(low, LANES - span, 1)
        high = high + pltpu.roll(high, span, 1)
        return jnp.where(low_lanes, low, high)

    def put(row, value):
        part_wide[pl.ds(row, pulsar_total, stride=apart_part), :] = value

    def settle(target):
        count = target.shape[1]
        for p in range(pulsar_total):
            target[p] = part_wide[p * apart_part : p * apart_part + count, :].astype(bf16)

    zero = jnp.zeros((pulsar_total, LANES), f32)

    def gather_own():
        diagonal = zero
        merged = []
        for j in range(side):
            if j >= half - side:
                merged.append(summed(own_grams, own_chosen, (j,))[0])
            else:
                first, second = summed(own_grams, own_chosen, (j, side + j))
                diagonal = diagonal + jnp.where(inner == side + j, second, 0.0)
                second = pltpu.roll(second, LANES - side, 1)
                merged.append(jnp.where((inner > j) & (inner < side), second, first))
        for j in range(quarter - 1):
            put(j, fold(merged[j], merged[j + quarter]))
        put(quarter - 1, fold(merged[quarter - 1], diagonal))
        put(quarter, projections())
        for row in range(quarter + 1, SHORT - 1):
            put(row, zero)
        put(SHORT - 1, places_ref[...])
        settle(own_part)

    def gather_cross():
        for r in range(side):
            slots = [j for j in (r, r + side) if j < half]
            found = summed(cross_grams, cross_chosen, slots) + [zero] * (2 - len(slots))
            put(r, fold(found[0], found[1]))
        for r in range(side, TALL):
            put(r, zero)
        settle(cross_part)

    def projections():
        terms = picked(own_grams, own_chosen, half)
        high = terms.astype(bf16)
        low = (terms - high.astype(f32)).astype(bf16)
        doubled = jnp.concatenate([own_chosen, own_chosen], axis=1)
        even, odd = joined(contract(doubled, jnp.concatenate([high, low], axis=0), ((1,), (0,))))
        value = fold(jnp.where(low_lanes, even, odd), zero)
        coarse = value.astype(bf16).astype(f32)
        return jnp.where(low_lanes, coarse, pltpu.roll(value - coarse, span, 1))

    def send_part(part, target, n):
        def one(k):
            e = jnp.where(k <= me, k - 1, k)
            d = jnp.where(k <= me, k - 1 - me + peers, k - me)
            pltpu.make_async_remote_copy(
                src_ref=part.at[pl.ds(e * owned, owned)],
                dst_ref=target.at[d],
                send_sem=sends.at[n],
                recv_sem=arrivals.at[n],
                device_id={"toa": e},
                device_id_type=MESH,
            ).start()

        each_peer(one)

    def total(part, target):
        mine = part[pl.ds(me * owned, owned)].astype(f32)
        return mine + jnp.sum(target[pl.ds(1, peers - 1)].astype(f32), axis=0)

    def own_chunks(keep, h):
        @pl.when(keep)
        def _():
            load(turn(2 * h + 1)).wait()

        @pl.when((h < steps // 2 - 1) & (2 * h + 2 >= swaps))
        def _():
            load(turn(2 * h + 2)).wait()

        own_chunk(2 * h, wide_even, wide_odd, keep)
        own_chunk(2 * h + 1, wide_odd, wide_even, keep)

    load(turn(0)).wait()
    spread(own_store, turn(0), wide_even)
    pl.semaphore_wait(barrier, peers)
    each_peer(send_rows)
    each(1, swaps, lambda p: load(turn(p)).wait())
    each(0, swaps, lambda g: swap(g).start())
    each(0, steps // 4, functools.partial(own_chunks, False))
    each(steps // 4, steps // 2, functools.partial(own_chunks, True))
    swap(0).wait_recv()
    swap(1).wait_recv()
    gather_own()
    cross_chunk(0)
    send_part(own_part, got_own, OWN)
    cross_chunk(1)

    for g in range(2, swaps):
        swap(g).wait_recv()
        cross_chunk(g)
    gather_cross()
    send_part(cross_part, got_cross, CROSS)

    def to_partner(source, target, n):
        return pltpu.make_async_remote_copy(
            src_ref=source,
            dst_ref=target,
            send_sem=sends.at[n],
            recv_sem=arrivals.at[n],
            device_id={"rep": partner},
            device_id_type=MESH,
        )

    arrived(got_cross, CROSS)
    cross_sum[...] = total(cross_part, got_cross)
    last = to_partner(cross_sum, partner_sum, LAST)
    last.start()
    everything = other_store
    pltpu.make_async_copy(everything, everything, sends.at[SWAP]).wait()
    arrived(got_rows, ROWS)
    arrived(got_own, OWN)
    own_sum = total(own_part, got_own)
    home = onehot(own_sum[0][SHORT - 1 : SHORT].astype(jnp.int32), tile_total)
    messages = got_rows[...].astype(f32)
    for c in range(cuts):
        rows = messages[:, c * per_peer : (c + 1) * per_peer, :].reshape(tile_total, LANES)
        white_ref[:, c * LANES : (c + 1) * LANES] = contract(
            home.astype(bf16), rows.astype(bf16), ((1,), (0,))
        )
    row_at = lax.broadcasted_iota(jnp.int32, (TALL, TALL), 0)
    lane_at = lax.broadcasted_iota(jnp.int32, (TALL, TALL), 1)
    place_at = lax.broadcasted_iota(jnp.int32, (span, LANES), 1)
    rest = half - side

    for q in range(owned):
        block = own_sum[q]
        high = pltpu.roll(block, LANES - span, 1)
        rows = [block[:quarter], high[: side - quarter], jnp.zeros((TALL - side, LANES), f32)]
        rows = jnp.concatenate(rows, axis=0)
        merged = rows[:, :TALL]
        mixed = rows[:, side : side + TALL]
        turned = jnp.transpose(merged)
        diagonal = high[quarter - 1 : quarter, side : side + TALL]
        upper = jnp.where(lane_at < row_at, turned, diagonal)
        upper = jnp.where(lane_at > row_at, merged, upper)
        lower = jnp.where(lane_at <= row_at, merged, turned)
        own_square[q, :side, :side] = lower[:side, :side]
        own_square[q, :side, side:half] = mixed[:side, :rest]
        own_square[q, side:half, :side] = jnp.transpose(mixed)[:rest, :side]
        own_square[q, side:half, side:half] = upper[:rest, :rest]
        square = own_square[q]
        own_square[q] = jnp.where(core == 0, square, pltpu.roll(square, half, 1))
        found = block[quarter : quarter + 1] + high[quarter : quarter + 1]
        projection_ref[q : q + 1, :] = found[:, :half]

    def unfold(block):
        tall = [block[:side, :span], block[:rest, span : 2 * span]]
        return jnp.concatenate(tall + [jnp.zeros((span - half, span), f32)], axis=0)

    last.wait()
    for q in range(owned):
        both = unfold(cross_sum[q]) + jnp.transpose(unfold(partner_sum[q]))
        both = jnp.concatenate([both, jnp.zeros((span, LANES - span), f32)], axis=1)
        both = jnp.where(core == 0, pltpu.roll(both, half, 1), both)
        mine = (place_at < half) == (core == 0)
        gram_ref[:, q, :] = jnp.where(mine, own_square[q], both)[:half, : 2 * half]
    for target, n in ((got_rows, ROWS), (got_own, OWN), (got_cross, CROSS)):
        gone(target, n)


def finish_kernel(gram_in, projection_in, white_in, gram_out, projection_out, white_out, sems):
    copies = [
        pltpu.make_async_copy(source, target, sems.at[n])
        for n, (source, target) in enumerate(
            [(white_in, white_out), (gram_in, gram_out), (projection_in, projection_out)]
        )
    ]
    for copy in copies:
        copy.start()
    for copy in copies:
        copy.wait()


def shards(
    residual, toa_error, basis_rows, efac_table, equad_table, pulsar, backend, counts, owner_slot
):
    tile_total, row_total = residual.shape
    peers = lax.axis_size("toa")
    half = basis_rows.shape[1]
    pulsar_total, backend_total = efac_table.shape
    owned = pulsar_total // peers
    per_peer = tile_total // peers
    group = min(GROUP, tile_total)
    steps = tile_total // group
    cuts = row_total // LANES
    span = round_up(half + 1, 8)
    message = round_up(cuts * per_peer, 16)
    f32 = jnp.float32
    bf16 = jnp.bfloat16
    i32 = jnp.int32
    anywhere = pl.BlockSpec(memory_space=pltpu.HBM)
    vmem = pl.BlockSpec(memory_space=pltpu.VMEM)

    def row(vector):
        return vector.reshape(1, tile_total)

    results = [
        ((half, owned, 2 * half), f32),
        ((owned, half), f32),
        ((tile_total, row_total), f32),
    ]
    held = pl.pallas_call(
        functools.partial(whole_kernel, peers),
        in_specs=[anywhere] * 9,
        out_specs=[vmem] * 3,
        out_shape=[pltpu.VMEM(shape, dtype) for shape, dtype in results],
        scratch_shapes=[
            pltpu.VMEM((1, tile_total), i32),
            pltpu.VMEM((1, tile_total), i32),
            pltpu.VMEM((1, tile_total), i32),
            pltpu.VMEM((1, tile_total), i32),
            pltpu.VMEM((pulsar_total, backend_total), f32),
            pltpu.VMEM((pulsar_total, backend_total), f32),
            pltpu.VMEM((tile_total, row_total), f32),
            pltpu.VMEM((tile_total, row_total), f32),
            pltpu.VMEM((peers, message, LANES), bf16),
            pltpu.VMEM((peers, message, LANES), bf16),
            pltpu.VMEM((pulsar_total, tile_total), f32),
            pltpu.VMEM((half, tile_total, row_total), bf16),
            pltpu.VMEM((half, tile_total // 2, row_total), bf16),
            pltpu.VMEM((tile_total, row_total), f32),
            pltpu.VMEM((cuts, span * PITCH, LANES), f32),
            pltpu.VMEM((cuts, span * PITCH, LANES), f32),
            pltpu.VMEM((tile_total // 4, 2 * span, row_total), bf16),
            pltpu.VMEM((tile_total // 2 * (span + 1), LANES), f32),
            pltpu.VMEM((tile_total // 4 * (span + 1), LANES), f32),
            pltpu.VMEM((pulsar_total * (TALL + 1), LANES), f32),
            pltpu.VMEM((pulsar_total, SHORT, LANES), bf16),
            pltpu.VMEM((pulsar_total, TALL, LANES), bf16),
            pltpu.VMEM((peers, owned, SHORT, LANES), bf16),
            pltpu.VMEM((peers, owned, TALL, LANES), bf16),
            pltpu.VMEM((owned, TALL, LANES), f32),
            pltpu.VMEM((owned, TALL, LANES), f32),
            pltpu.VMEM((owned, span, LANES), f32),
            pltpu.SemaphoreType.DMA((8,)),
            pltpu.SemaphoreType.DMA((steps,)),
            pltpu.SemaphoreType.DMA((steps // 2,)),
            pltpu.SemaphoreType.DMA((5,)),
            pltpu.SemaphoreType.DMA((5,)),
        ],
        compiler_params=pltpu.CompilerParams(
            collective_id=0, has_side_effects=True, vmem_limit_bytes=VMEM_KERNEL
        ),
        name="whole",
    )(
        *[
            pltpu.with_memory_space_constraint(value, pltpu.HBM)
            for value in (
                row(pulsar),
                row(backend),
                row(counts),
                row(owner_slot),
                efac_table,
                equad_table,
                residual,
                toa_error,
                jnp.transpose(basis_rows, (1, 0, 2)),
            )
        ]
    )
    gram, projection, whitened = pl.pallas_call(
        finish_kernel,
        in_specs=[vmem] * 3,
        out_specs=[anywhere] * 3,
        out_shape=[jax.ShapeDtypeStruct(shape, dtype) for shape, dtype in results],
        scratch_shapes=[pltpu.SemaphoreType.DMA((3,))],
        name="finish",
    )(*[pltpu.with_memory_space_constraint(value, pltpu.VMEM) for value in held])
    return (jnp.transpose(gram, (1, 2, 0)), projection, whitened)


def solution(mesh):
    in_specs = (
        P("toa", None),
        P("toa", None),
        P("toa", "rep", None),
        P(),
        P(),
        P("toa"),
        P("toa"),
        P("toa"),
        P("toa"),
    )
    out_specs = (P("toa", None, "rep"), P("toa", "rep"), P("toa", None))
    return jax.shard_map(shards, mesh=mesh, in_specs=in_specs, out_specs=out_specs, check_vma=False)
```

```python
import functools

import jax
import jax.numpy as jnp
from jax import lax
from jax.experimental import pallas as pl
from jax.experimental.pallas import tpu as pltpu
from jax.sharding import PartitionSpec as P

MESH = pl.DeviceIdType.MESH
GROUP = 16
BURST = 15
LANES = 128
PITCH = GROUP + 1
SHORT = 16
TALL = 32
VMEM_KERNEL = 48 * 1024 * 1024
SWAP, ROWS, OWN, CROSS, LAST = range(5)


def round_up(value, step):
    return (value + step - 1) // step * step


def contract(left, right, dims):
    return lax.dot_general(
        left, right, (dims, ((), ())), preferred_element_type=jnp.float32
    )


def whole_kernel(
    peers,
    pulsar_hbm,
    backend_hbm,
    counts_hbm,
    slot_hbm,
    efac_hbm,
    equad_hbm,
    residual_hbm,
    error_hbm,
    basis_ref,
    gram_ref,
    projection_ref,
    white_ref,
    pulsar_ref,
    backend_ref,
    counts_ref,
    slot_ref,
    efac_ref,
    equad_ref,
    residual_ref,
    error_ref,
    sorted_rows,
    got_rows,
    places_ref,
    own_store,
    other_store,
    weights,
    wide_even,
    wide_odd,
    lefts,
    own_grams,
    cross_grams,
    part_wide,
    own_part,
    cross_part,
    got_own,
    got_cross,
    cross_sum,
    partner_sum,
    own_square,
    small_sems,
    load_sems,
    swap_arrivals,
    sends,
    arrivals,
):
    me = lax.axis_index("toa")
    core = lax.axis_index("rep")
    partner = 1 - core
    half, tile_total, row_total = basis_ref.shape
    pulsar_total = efac_hbm.shape[0]
    owned = pulsar_total // peers
    per_peer = tile_total // peers
    group = min(GROUP, tile_total)
    steps = tile_total // group
    swaps = steps // 2
    cuts = row_total // LANES
    side = (half + 1) // 2
    quarter = (side + 1) // 2
    span = round_up(half + 1, 8)
    apart = span + 1
    apart_part = TALL + 1
    f32 = jnp.float32
    bf16 = jnp.bfloat16

    barrier = pltpu.get_barrier_semaphore()
    pl.semaphore_signal(barrier, inc=1, device_id={"rep": partner}, device_id_type=MESH)

    def each(first, last, action):
        def body(i, carry):
            action(i)
            return carry

        lax.fori_loop(first, last, body, 0)

    def each_peer(action):
        step = BURST if (peers - 1) % BURST == 0 else 1

        def burst(i):
            for k in range(step):
                action(1 + i * step + k)

        each(0, (peers - 1) // step, burst)

    def greet(d):
        pl.semaphore_signal(
            barrier, inc=1, device_id={"toa": lax.rem(me + d, peers)}, device_id_type=MESH
        )


    small = [
        pltpu.make_async_copy(source, target, small_sems.at[n])
        for n, (source, target) in enumerate(
            [
                (pulsar_hbm, pulsar_ref),
                (backend_hbm, backend_ref),
                (efac_hbm, efac_ref),
                (equad_hbm, equad_ref),
                (counts_hbm, counts_ref),
                (slot_hbm, slot_ref),
                (error_hbm, error_ref),
                (residual_hbm, residual_ref),
            ]
        )
    ]
    for copy in small:
        copy.start()
    each_peer(greet)

    def chunk(ref, g):
        return ref.at[:, pl.ds(pl.multiple_of(g * group, group), group), :]

    def load(g):
        return pltpu.make_async_copy(chunk(basis_ref, g), chunk(own_store, g), load_sems.at[g])

    def turn(p):
        return lax.rem(partner * swaps + p, steps)

    each(0, steps, lambda p: load(turn(p)).start())

    def swap(g):
        return pltpu.make_async_remote_copy(
            src_ref=chunk(own_store, partner * swaps + g),
            dst_ref=chunk(other_store, g),
            send_sem=sends.at[SWAP],
            recv_sem=swap_arrivals.at[g],
            device_id={"rep": partner},
            device_id_type=MESH,
        )


    for wide in (wide_even, wide_odd):
        for c in range(cuts):
            wide[c, half * PITCH :, :] = jnp.zeros(((span - half) * PITCH, LANES), f32)
    for copy in small[:-2]:
        copy.wait()

    def onehot(row, amount):
        index = lax.broadcasted_iota(jnp.int32, (amount, row.shape[1]), 0)
        return (index == row).astype(f32)

    pulsar_hot = onehot(pulsar_ref[...], pulsar_total)
    backend_hot = onehot(backend_ref[...], efac_ref.shape[1])

    def terms_of(values):
        high = values.astype(bf16)
        rest = values - high.astype(f32)
        middle = rest.astype(bf16)
        return [high, middle, (rest - middle.astype(f32)).astype(bf16)]

    def lookup(ref):
        table = jnp.concatenate(terms_of(ref[...]), axis=0)
        hot = jnp.concatenate([pulsar_hot.astype(bf16)] * 3, axis=0)
        columns = contract(table, hot, ((0,), (0,)))
        return jnp.sum(columns * backend_hot, axis=0, keepdims=True)

    factor = lookup(efac_ref)
    floor_term = lookup(equad_ref)
    stacked = jnp.concatenate(
        [
            factor * factor,
            floor_term * floor_term,
            counts_ref[...].astype(f32),
            jnp.zeros((5, tile_total), f32),
        ],
        axis=0,
    )
    columns = jnp.transpose(stacked)
    slot = slot_ref[...]
    dest = slot // tile_total
    place = (slot - dest * tile_total).astype(f32)
    dest_hot = onehot(dest, peers)
    earlier = (
        lax.broadcasted_iota(jnp.int32, (tile_total, tile_total), 0)
        < lax.broadcasted_iota(jnp.int32, (tile_total, tile_total), 1)
    ).astype(bf16)
    before = contract(dest_hot.astype(bf16), earlier, ((1,), (0,)))
    rank = jnp.sum(before * dest_hot, axis=0, keepdims=True)
    position = lax.rem(dest - me + peers, peers) * per_peer + rank.astype(jnp.int32)
    order = onehot(position, tile_total).astype(bf16)
    places = contract((dest_hot * place).astype(bf16), order, ((1,), (1,)))
    places_ref[...] = jnp.repeat(places, owned, axis=0) if owned > 1 else places

    evens = lax.broadcasted_iota(jnp.int32, (tile_total, tile_total), 0)
    pairs = lax.broadcasted_iota(jnp.int32, (tile_total, tile_total), 1)
    count = tile_total // 2
    halves = jnp.where(pairs < count, 2 * pairs, 2 * (pairs - count) + 1)
    parted = contract(pulsar_hot.astype(bf16), (evens == halves).astype(bf16), ((1,), (0,)))
    parted = parted.astype(bf16)
    own_chosen = jnp.concatenate([parted[:, :count], parted[:, count:]], axis=0)
    cross_chosen = jnp.where(core == 0, own_chosen[:, : count // 2], own_chosen[:, count // 2 :])
    for copy in small[-2:]:
        copy.wait()
    lane = lax.broadcasted_iota(jnp.int32, (tile_total, row_total), 1).astype(f32)
    error = error_ref[...]
    weight = jnp.where(
        lane < columns[:, 2:3], 1.0 / (columns[:, 0:1] * (error * error) + columns[:, 1:2]), 0.0
    )
    weights[...] = weight

    white = jnp.sqrt(weight) * residual_ref[...]
    ordered = contract(order, white.astype(bf16), ((1,), (0,)))
    ordered = ordered.reshape(peers, per_peer, row_total)
    pieces = [ordered[:, :, c * LANES : (c + 1) * LANES] for c in range(cuts)]
    unused = sorted_rows.shape[1] - cuts * per_peer
    if unused:
        pieces.append(jnp.zeros((peers, unused, LANES), f32))
    message = jnp.concatenate(pieces, axis=1).astype(bf16)
    sorted_rows[...] = message
    got_rows[0] = message[0]

    def remote(source, target, n, d):
        return pltpu.make_async_remote_copy(
            src_ref=source,
            dst_ref=target.at[d],
            send_sem=sends.at[n],
            recv_sem=arrivals.at[n],
            device_id={"toa": lax.rem(me + d, peers)},
            device_id_type=MESH,
        )

    def arrived(target, n):
        rest = target.at[pl.ds(1, peers - 1)]
        pltpu.make_async_copy(rest, rest, arrivals.at[n]).wait()

    def gone(target, n):
        rest = target.at[pl.ds(1, peers - 1)]
        pltpu.make_async_copy(rest, rest, sends.at[n]).wait()

    def send_rows(d):
        remote(sorted_rows.at[d], got_rows, ROWS, d).start()


    def spread(ref, g, wide, piece=0, pieces=1):
        start = pl.multiple_of(g * group, group)
        for j in range(half * piece // pieces, half * (piece + 1) // pieces):
            block = ref[j, pl.ds(start, group), :].astype(f32)
            at = j * PITCH
            for c in range(cuts):
                wide[c, at : at + group, :] = block[:, c * LANES : (c + 1) * LANES]

    def columns_of(wide, i):
        return jnp.concatenate(
            [wide[c, pl.ds(i, span, stride=PITCH), :] for c in range(cuts)], axis=1
        )

    starts = half // 8 * 8
    below = lax.broadcasted_iota(jnp.int32, (span - starts, row_total), 0) == half - starts
    first_lanes = lax.broadcasted_iota(jnp.int32, (span, 2 * span), 1) < span
    unused_lanes = jnp.zeros((span, LANES - 2 * span), f32)

    def multiply(grams, g, step, left, right):
        both = contract(left, right, ((1,), (1,)))
        both = jnp.where(first_lanes, both[:span], both[span:])
        row = pl.multiple_of(g * (group // 2 * apart), 8) + step * apart
        grams[pl.ds(row, span), :] = jnp.concatenate([both, unused_lanes], axis=1)

    def own_chunk(p, wide, other, keep):
        g = turn(p)
        later = turn(jnp.minimum(p + 1, steps - 1))
        start = pl.multiple_of(g * group, group)
        weight = weights[pl.ds(start, group), :]
        residual = residual_ref[pl.ds(start, group), :]
        spread(own_store, later, other)
        for i in range(0, group, 2):
            bases = [columns_of(wide, k) for k in (i, i + 1)]
            scaled = []
            for k, basis in zip((i, i + 1), bases):
                with_residual = jnp.where(below, residual[k : k + 1, :], basis[starts:])
                one = jnp.concatenate([basis[:starts], with_residual], axis=0)
                scaled.append(weight[k : k + 1, :] * one)
            left = jnp.concatenate(scaled, axis=0).astype(bf16)
            if keep:
                lefts[(p - swaps) * (group // 2) + i // 2] = left
            right = jnp.concatenate(bases, axis=0).astype(bf16)
            multiply(own_grams, g, i // 2, left, right)

    def cross_chunk(g):
        spread(other_store, g, wide_even)
        for i in range(0, group, 2):
            bases = [columns_of(wide_even, k) for k in (i, i + 1)]
            right = jnp.concatenate(bases, axis=0).astype(bf16)
            multiply(cross_grams, g, i // 2, lefts[g * (group // 2) + i // 2], right)

    lanes = lax.broadcasted_iota(jnp.int32, (pulsar_total, LANES), 1)
    low_lanes = lanes < span
    inner = jnp.where(low_lanes, lanes, lanes - span)

    def picked(grams, chosen, j):
        return grams[pl.ds(j, chosen.shape[1], stride=apart), :]

    def joined(out):
        return out[:pulsar_total], out[pulsar_total:]

    def summed(grams, chosen, slots):
        sides = [picked(grams, chosen, slot).astype(bf16) for slot in slots]
        even, odd = joined(contract(chosen, jnp.concatenate(sides, axis=1), ((1,), (0,))))
        return [
            jnp.where(low_lanes, even[:, at : at + LANES], odd[:, at : at + LANES])
            for at in range(0, len(slots) * LANES, LANES)
        ]

    def fold(low, high):
        low = low + pltpu.roll(low, LANES - span, 1)
        high = high + pltpu.roll(high, span, 1)
        return jnp.where(low_lanes, low, high)

    def put(row, value):
        part_wide[pl.ds(row, pulsar_total, stride=apart_part), :] = value

    def settle(target):
        count = target.shape[1]
        for p in range(pulsar_total):
            target[p] = part_wide[p * apart_part : p * apart_part + count, :].astype(bf16)

    zero = jnp.zeros((pulsar_total, LANES), f32)

    def gather_own():
        diagonal = zero
        merged = []
        for j in range(side):
            if j >= half - side:
                merged.append(summed(own_grams, own_chosen, (j,))[0])
            else:
                first, second = summed(own_grams, own_chosen, (j, side + j))
                diagonal = diagonal + jnp.where(inner == side + j, second, 0.0)
                second = pltpu.roll(second, LANES - side, 1)
                merged.append(jnp.where((inner > j) & (inner < side), second, first))
        for j in range(quarter - 1):
            put(j, fold(merged[j], merged[j + quarter]))
        put(quarter - 1, fold(merged[quarter - 1], diagonal))
        put(quarter, projections())
        for row in range(quarter + 1, SHORT - 1):
            put(row, zero)
        put(SHORT - 1, places_ref[...])
        settle(own_part)

    def gather_cross():
        for r in range(side):
            slots = [j for j in (r, r + side) if j < half]
            found = summed(cross_grams, cross_chosen, slots) + [zero] * (2 - len(slots))
            put(r, fold(found[0], found[1]))
        for r in range(side, TALL):
            put(r, zero)
        settle(cross_part)

    def projections():
        terms = picked(own_grams, own_chosen, half)
        high = terms.astype(bf16)
        low = (terms - high.astype(f32)).astype(bf16)
        doubled = jnp.concatenate([own_chosen, own_chosen], axis=1)
        even, odd = joined(contract(doubled, jnp.concatenate([high, low], axis=0), ((1,), (0,))))
        value = fold(jnp.where(low_lanes, even, odd), zero)
        coarse = value.astype(bf16).astype(f32)
        return jnp.where(low_lanes, coarse, pltpu.roll(value - coarse, span, 1))

    def send_part(part, target, n):
        def one(k):
            e = jnp.where(k <= me, k - 1, k)
            d = jnp.where(k <= me, k - 1 - me + peers, k - me)
            pltpu.make_async_remote_copy(
                src_ref=part.at[pl.ds(e * owned, owned)],
                dst_ref=target.at[d],
                send_sem=sends.at[n],
                recv_sem=arrivals.at[n],
                device_id={"toa": e},
                device_id_type=MESH,
            ).start()

        each_peer(one)

    def total(part, target):
        mine = part[pl.ds(me * owned, owned)].astype(f32)
        return mine + jnp.sum(target[pl.ds(1, peers - 1)].astype(f32), axis=0)

    def own_chunks(keep, h):
        @pl.when(keep)
        def _():
            load(turn(2 * h + 1)).wait()

        @pl.when((h < steps // 2 - 1) & (2 * h + 2 >= swaps))
        def _():
            load(turn(2 * h + 2)).wait()

        own_chunk(2 * h, wide_even, wide_odd, keep)
        own_chunk(2 * h + 1, wide_odd, wide_even, keep)

    load(turn(0)).wait()
    spread(own_store, turn(0), wide_even)
    pl.semaphore_wait(barrier, peers)
    each_peer(send_rows)
    each(1, swaps, lambda p: load(turn(p)).wait())
    each(0, swaps, lambda g: swap(g).start())
    for h in range(steps // 2):
        own_chunks(h >= steps // 4, h)
    swap(0).wait_recv()
    gather_own()
    cross_chunk(0)
    send_part(own_part, got_own, OWN)

    for g in range(1, swaps):
        swap(g).wait_recv()
        cross_chunk(g)
    gather_cross()
    send_part(cross_part, got_cross, CROSS)

    def to_partner(source, target, n):
        return pltpu.make_async_remote_copy(
            src_ref=source,
            dst_ref=target,
            send_sem=sends.at[n],
            recv_sem=arrivals.at[n],
            device_id={"rep": partner},
            device_id_type=MESH,
        )

    arrived(got_cross, CROSS)
    cross_sum[...] = total(cross_part, got_cross)
    last = to_partner(cross_sum, partner_sum, LAST)
    last.start()
    everything = other_store
    pltpu.make_async_copy(everything, everything, sends.at[SWAP]).wait()
    arrived(got_rows, ROWS)
    arrived(got_own, OWN)
    own_sum = total(own_part, got_own)
    home = onehot(own_sum[0][SHORT - 1 : SHORT].astype(jnp.int32), tile_total)
    messages = got_rows[...].astype(f32)
    for c in range(cuts):
        rows = messages[:, c * per_peer : (c + 1) * per_peer, :].reshape(tile_total, LANES)
        white_ref[:, c * LANES : (c + 1) * LANES] = contract(
            home.astype(bf16), rows.astype(bf16), ((1,), (0,))
        )
    row_at = lax.broadcasted_iota(jnp.int32, (TALL, TALL), 0)
    lane_at = lax.broadcasted_iota(jnp.int32, (TALL, TALL), 1)
    place_at = lax.broadcasted_iota(jnp.int32, (span, LANES), 1)
    rest = half - side

    for q in range(owned):
        block = own_sum[q]
        high = pltpu.roll(block, LANES - span, 1)
        rows = [block[:quarter], high[: side - quarter], jnp.zeros((TALL - side, LANES), f32)]
        rows = jnp.concatenate(rows, axis=0)
        merged = rows[:, :TALL]
        mixed = rows[:, side : side + TALL]
        turned = jnp.transpose(merged)
        diagonal = high[quarter - 1 : quarter, side : side + TALL]
        upper = jnp.where(lane_at < row_at, turned, diagonal)
        upper = jnp.where(lane_at > row_at, merged, upper)
        lower = jnp.where(lane_at <= row_at, merged, turned)
        own_square[q, :side, :side] = lower[:side, :side]
        own_square[q, :side, side:half] = mixed[:side, :rest]
        own_square[q, side:half, :side] = jnp.transpose(mixed)[:rest, :side]
        own_square[q, side:half, side:half] = upper[:rest, :rest]
        square = own_square[q]
        own_square[q] = jnp.where(core == 0, square, pltpu.roll(square, half, 1))
        found = block[quarter : quarter + 1] + high[quarter : quarter + 1]
        projection_ref[q : q + 1, :] = found[:, :half]

    def unfold(block):
        tall = [block[:side, :span], block[:rest, span : 2 * span]]
        return jnp.concatenate(tall + [jnp.zeros((span - half, span), f32)], axis=0)

    for target, n in ((got_rows, ROWS), (got_own, OWN), (got_cross, CROSS)):
        gone(target, n)
    last.wait()
    for q in range(owned):
        both = unfold(cross_sum[q]) + jnp.transpose(unfold(partner_sum[q]))
        both = jnp.concatenate([both, jnp.zeros((span, LANES - span), f32)], axis=1)
        both = jnp.where(core == 0, pltpu.roll(both, half, 1), both)
        mine = (place_at < half) == (core == 0)
        gram_ref[:, q, :] = jnp.where(mine, own_square[q], both)[:half, : 2 * half]


def finish_kernel(gram_in, projection_in, white_in, gram_out, projection_out, white_out, sems):
    copies = [
        pltpu.make_async_copy(source, target, sems.at[n])
        for n, (source, target) in enumerate(
            [(white_in, white_out), (gram_in, gram_out), (projection_in, projection_out)]
        )
    ]
    for copy in copies:
        copy.start()
    for copy in copies:
        copy.wait()


def shards(
    residual, toa_error, basis_rows, efac_table, equad_table, pulsar, backend, counts, owner_slot
):
    tile_total, row_total = residual.shape
    peers = lax.axis_size("toa")
    half = basis_rows.shape[1]
    pulsar_total, backend_total = efac_table.shape
    owned = pulsar_total // peers
    per_peer = tile_total // peers
    group = min(GROUP, tile_total)
    steps = tile_total // group
    cuts = row_total // LANES
    span = round_up(half + 1, 8)
    message = round_up(cuts * per_peer, 16)
    f32 = jnp.float32
    bf16 = jnp.bfloat16
    i32 = jnp.int32
    anywhere = pl.BlockSpec(memory_space=pltpu.HBM)
    vmem = pl.BlockSpec(memory_space=pltpu.VMEM)

    def row(vector):
        return vector.reshape(1, tile_total)

    results = [
        ((half, owned, 2 * half), f32),
        ((owned, half), f32),
        ((tile_total, row_total), f32),
    ]
    held = pl.pallas_call(
        functools.partial(whole_kernel, peers),
        in_specs=[anywhere] * 9,
        out_specs=[vmem] * 3,
        out_shape=[pltpu.VMEM(shape, dtype) for shape, dtype in results],
        scratch_shapes=[
            pltpu.VMEM((1, tile_total), i32),
            pltpu.VMEM((1, tile_total), i32),
            pltpu.VMEM((1, tile_total), i32),
            pltpu.VMEM((1, tile_total), i32),
            pltpu.VMEM((pulsar_total, backend_total), f32),
            pltpu.VMEM((pulsar_total, backend_total), f32),
            pltpu.VMEM((tile_total, row_total), f32),
            pltpu.VMEM((tile_total, row_total), f32),
            pltpu.VMEM((peers, message, LANES), bf16),
            pltpu.VMEM((peers, message, LANES), bf16),
            pltpu.VMEM((pulsar_total, tile_total), f32),
            pltpu.VMEM((half, tile_total, row_total), bf16),
            pltpu.VMEM((half, tile_total // 2, row_total), bf16),
            pltpu.VMEM((tile_total, row_total), f32),
            pltpu.VMEM((cuts, span * PITCH, LANES), f32),
            pltpu.VMEM((cuts, span * PITCH, LANES), f32),
            pltpu.VMEM((tile_total // 4, 2 * span, row_total), bf16),
            pltpu.VMEM((tile_total // 2 * (span + 1), LANES), f32),
            pltpu.VMEM((tile_total // 4 * (span + 1), LANES), f32),
            pltpu.VMEM((pulsar_total * (TALL + 1), LANES), f32),
            pltpu.VMEM((pulsar_total, SHORT, LANES), bf16),
            pltpu.VMEM((pulsar_total, TALL, LANES), bf16),
            pltpu.VMEM((peers, owned, SHORT, LANES), bf16),
            pltpu.VMEM((peers, owned, TALL, LANES), bf16),
            pltpu.VMEM((owned, TALL, LANES), f32),
            pltpu.VMEM((owned, TALL, LANES), f32),
            pltpu.VMEM((owned, span, LANES), f32),
            pltpu.SemaphoreType.DMA((8,)),
            pltpu.SemaphoreType.DMA((steps,)),
            pltpu.SemaphoreType.DMA((steps // 2,)),
            pltpu.SemaphoreType.DMA((5,)),
            pltpu.SemaphoreType.DMA((5,)),
        ],
        compiler_params=pltpu.CompilerParams(
            collective_id=0, has_side_effects=True, vmem_limit_bytes=VMEM_KERNEL
        ),
        name="whole",
    )(
        *[
            pltpu.with_memory_space_constraint(value, pltpu.HBM)
            for value in (
                row(pulsar),
                row(backend),
                row(counts),
                row(owner_slot),
                efac_table,
                equad_table,
                residual,
                toa_error,
                jnp.transpose(basis_rows, (1, 0, 2)),
            )
        ]
    )
    gram, projection, whitened = pl.pallas_call(
        finish_kernel,
        in_specs=[vmem] * 3,
        out_specs=[anywhere] * 3,
        out_shape=[jax.ShapeDtypeStruct(shape, dtype) for shape, dtype in results],
        scratch_shapes=[pltpu.SemaphoreType.DMA((3,))],
        name="finish",
    )(*[pltpu.with_memory_space_constraint(value, pltpu.VMEM) for value in held])
    return (jnp.transpose(gram, (1, 2, 0)), projection, whitened)


def solution(mesh):
    in_specs = (
        P("toa", None),
        P("toa", None),
        P("toa", "rep", None),
        P(),
        P(),
        P("toa"),
        P("toa"),
        P("toa"),
        P("toa"),
    )
    out_specs = (P("toa", None, "rep"), P("toa", "rep"), P("toa", None))
    return jax.shard_map(shards, mesh=mesh, in_specs=in_specs, out_specs=out_specs, check_vma=False)
```
